768 devices in a mesh: depth: 8 (over y), plane: 96 (over x, z, core).
Axes of the slice: x: 4, y: 8, z: 12, core: 2. Of those that a mesh axis runs over, the one named last changes fastest.
Arguments:
- density: bfloat16 [128, 768, 1536], P('depth', 'plane'), may hold values from -6 to 6
- material: int32 [128, 768, 1536], P('depth', 'plane'), may hold values from 0 to 15
- tf_color: float32 [3, 16], replicated, may hold values from 0.2 to 1
- tf_extinction: float32 [16], replicated, may hold values from 0.5 to 8
Outputs:
- image: float32 [4, 768, 1536], P(None, 'plane', 'depth')
The draws below stay inside these ranges and needn't reach their ends.
All inputs are finite; a program needn't handle non-finite values.
Results may differ from the reference program's by a relative error of at most 0.0003.
Values may be sent and summed in bfloat16 or wider, within the bound.
A program may use at most 32 MiB of HBM per device.

```python
import math
import jax
import jax.numpy as jnp
from jax import lax

NY = 1536
LEVELS = 16
NZ = 128
NX = 768


def plant(result, rng, least, top_value):
    shape = result.shape
    index_at = [jax.random.randint(jax.random.fold_in(rng, axis), (), 0, shape[axis]) for axis in range(len(shape))]
    result = result.at[tuple(index_at)].set(least)
    longest = shape.index(max(shape))
    index_at[longest] = (index_at[longest] + 1) % shape[longest]
    return result.at[tuple(index_at)].set(top_value)


def block_scale(rng, extent, split, smallest, top_value):
    def one(dim, shards_of):
        draws = jax.random.uniform(jax.random.fold_in(jax.random.fold_in(rng, 6), dim), (shards_of,), jnp.float32, smallest / len(split), top_value / len(split))
        return jnp.repeat(jnp.exp(draws), extent[dim] // shards_of).reshape((-1,) + (1,) * (len(extent) - dim - 1))

    gain = one(*split[0])
    for cut in split[1:]:
        gain = gain * one(*cut)
    return gain


def scatter_about(rng, extent, deviation, bound, split=(), held_as=jnp.bfloat16):
    loudness = block_scale(rng, extent, split, -0.22, 0.18) if split else 1.0
    array = jax.random.normal(rng, extent, jnp.float32) * deviation * loudness
    return jnp.minimum(jnp.maximum(array, -bound), bound).astype(held_as)


def setup_inputs(seed: int = 0) -> dict:
    key_of = jax.random.split(jax.random.key(seed), 5)
    density = scatter_about(key_of[0], (NZ, NX, NY), 1.0, 6.0, ((0, 8), (1, 96)))
    material = plant(jax.random.randint(key_of[1], (NZ, NX, NY), 0, LEVELS), jax.random.fold_in(key_of[1], 1), 0, LEVELS - 1).astype(jnp.int32)
    tf_color = jnp.clip(jax.random.uniform(key_of[2], (3, LEVELS), jnp.float32, 0.2, 1.0), 0.2, 1.0)
    tf_extinction = jnp.clip(jnp.exp(jax.random.uniform(key_of[3], (LEVELS,), jnp.float32, math.log(0.5), math.log(8.0))), 0.5, 8.0)
    return dict(density=density, material=material, tf_color=tf_color, tf_extinction=tf_extinction)


light_z = 0.64
light_x = 0.48
light_y = 0.6

def tent_valid(field, axis):
    count = field.shape[axis]
    left = lax.slice_in_dim(field, 0, count - 2, axis=axis)
    middle = lax.slice_in_dim(field, 1, count - 1, axis=axis)
    right = lax.slice_in_dim(field, 2, count, axis=axis)
    return (left + 2.0 * middle + right) * 0.25

def slope_valid(field, axis):
    count = field.shape[axis]
    left = lax.slice_in_dim(field, 0, count - 2, axis=axis)
    right = lax.slice_in_dim(field, 2, count, axis=axis)
    return (right - left) * 0.5

def pad_last(field):
    return jnp.pad(field, ((0, 0), (0, 0), (1, 1)))

def render_block(smooth_ext, labels, tf_color, tf_extinction, scale):
    smooth = smooth_ext[1:-1, 1:-1]
    grad_z = slope_valid(tent_valid(pad_last(tent_valid(smooth_ext, 1)), 2), 0)
    grad_x = slope_valid(tent_valid(pad_last(tent_valid(smooth_ext, 0)), 2), 1)
    grad_y = slope_valid(pad_last(tent_valid(tent_valid(smooth_ext, 0), 1)), 2)
    lit = 0.35 + 0.65 * jnp.abs(light_z * grad_z + light_x * grad_x + light_y * grad_y) / jnp.sqrt(grad_z * grad_z + grad_x * grad_x + grad_y * grad_y + 1.0)
    optical = tf_extinction[labels] * (smooth * smooth + 0.25) * scale
    running = jnp.cumsum(optical, axis=0)
    weight = jnp.exp(-(running - optical)) * (1.0 - jnp.exp(-optical)) * lit
    colors = [lax.optimization_barrier(jnp.sum(weight * tf_color[channel][labels], axis=0)) for channel in range(3)]
    alpha = 1.0 - jnp.exp(-running[-1])
    return jnp.stack(colors + [alpha], axis=0)

def reference(density, material, tf_color, tf_extinction):
    block_rows = math.gcd(NX, 8)
    padded = jnp.pad(density, ((2, 2), (2, 2), (0, 0)))
    scale = 2.0 / NZ

    def one_block(start):
        slab = lax.dynamic_slice_in_dim(padded, start, block_rows + 4, 1).astype(jnp.float32)
        smooth = tent_valid(pad_last(tent_valid(tent_valid(slab, 0), 1)), 2)
        zpos = jnp.arange(NZ + 2, dtype=jnp.int32) - 1
        xpos = start + jnp.arange(block_rows + 2, dtype=jnp.int32) - 1
        inside = ((zpos >= 0) & (zpos < NZ))[:, None, None] & ((xpos >= 0) & (xpos < NX))[None, :, None]
        smooth = jnp.where(inside, smooth, jnp.float32(0.0))
        labels = lax.dynamic_slice_in_dim(material, start, block_rows, 1)
        return render_block(smooth, labels, tf_color, tf_extinction, scale)
    starts = (jnp.arange(NX // block_rows, dtype=jnp.int32) * block_rows).astype(jnp.int32)
    blocks = lax.map(one_block, starts)
    return jnp.transpose(blocks, (1, 0, 2, 3)).reshape(4, NX, NY)
```

```python
import functools

import jax
import jax.numpy as jnp
import numpy as np
from jax import lax
from jax.experimental import pallas as pl
from jax.experimental.pallas import tpu as pltpu
from jax.sharding import PartitionSpec as P

LIGHT_Z = 0.64
LIGHT_X = 0.48
LIGHT_Y = 0.6
LANES = 128
MESH = pl.DeviceIdType.MESH

TENT = np.array([0.0, 1.0, 2.0, 1.0, 0.0]) / 4.0
TENT_TENT = np.array([1.0, 4.0, 6.0, 4.0, 1.0]) / 16.0
SLOPE_TENT = np.array([-1.0, -2.0, 0.0, 2.0, 1.0]) / 8.0
RESULTS = (
    (TENT, TENT, 1.0 / 4.0),
    (SLOPE_TENT, TENT_TENT, 1.0 / 16.0),
    (TENT_TENT, SLOPE_TENT, 1.0 / 16.0),
    (TENT_TENT, TENT_TENT, 1.0 / 8.0),
)


def banded(taps, count, case):
    matrix = np.zeros((count, count + 4))
    for o in range(count):
        matrix[o, o : o + 5] = taps
    if case == 0:
        matrix[:, 2] -= matrix[:, 0]
        matrix[:, 0:2] = 0.0
    if case == 2:
        matrix[:, count + 1] -= matrix[:, count + 3]
        matrix[:, count + 2 : count + 4] = 0.0
    return matrix


def halo_rows(zs, xs):
    rows = [(z + 2, x + 2) for z in range(zs) for x in range(xs)]
    rows += [(z, x + 2) for z in (0, 1) for x in range(xs)]
    rows += [(zs + 2 + z, x + 2) for z in (0, 1) for x in range(xs)]
    rows += [(z + 2, x) for z in range(zs) for x in (0, 1)]
    rows += [(z + 2, xs + 2 + x) for z in range(zs) for x in (0, 1)]
    for z0 in (0, zs + 2):
        for x0 in (0, xs + 2):
            rows += [(z0 + z, x0 + x) for z in (0, 1) for x in (0, 1)]
            rows += [(-1, -1)] * 4
    return rows


def tables(zs, xs):
    rows = halo_rows(zs, xs)
    zi = np.array([r[0] for r in rows])
    xi = np.array([r[1] for r in rows])
    keep = (zi >= 0).astype(np.float64)
    zi, xi = np.maximum(zi, 0), np.maximum(xi, 0)
    ztab = np.stack(
        [
            np.concatenate([banded(z_taps, zs, case)[:, zi] for z_taps, _, _ in RESULTS])
            for case in range(3)
        ]
    )
    xtab = np.stack(
        [
            np.concatenate(
                [banded(x_taps, xs, case)[:, xi] * keep * scale for _, x_taps, scale in RESULTS]
            )
            for case in range(3)
        ]
    )
    return ztab.astype(np.float32), xtab.astype(np.float32)


def edge_picker(zs, xs):
    own = {(z, x): z * xs + x for z in range(zs) for x in range(xs)}
    wanted = [own[z, x] for z in range(zs) for x in (0, 1)]
    wanted += [own[z, x] for z in range(zs) for x in (xs - 2, xs - 1)]
    for z0 in (0, zs - 2):
        for x0 in (0, xs - 2):
            wanted += [own[z0 + z, x0 + x] for z in (0, 1) for x in (0, 1)]
            wanted += [-1] * 4
    picker = np.zeros((len(wanted), zs * xs), np.float32)
    for row, source in enumerate(wanted):
        if source >= 0:
            picker[row, source] = 1.0
    return picker


def frame_kernel(
    zs, xs, cols, bricks, planes,
    dens_hbm, mat_hbm, color_ref, ext_ref, ztab_hbm, xtab_hbm, pick_hbm,
    out_ref,
    field, mats, ztab, xtab, pick, edges, taps, filtered, looked, lut, send, recv,
    load_sem, halo_send, halo_recv, part_send, part_recv,
):
    own = zs * xs
    me_z = lax.axis_index("depth")
    me_x = lax.axis_index("plane")

    def move(src, dst, sem):
        return pltpu.make_async_copy(src, dst, load_sem.at[sem])

    z_case = jnp.where(me_z == 0, 0, jnp.where(me_z == bricks - 1, 2, 1))
    x_case = jnp.where(me_x == 0, 0, jnp.where(me_x == planes - 1, 2, 1))
    loads = [
        move(dens_hbm, field.at[0:own, pl.ds(LANES, cols)], 0),
        move(pick_hbm, pick, 1),
        move(mat_hbm, mats, 2),
        move(ztab_hbm.at[z_case], ztab, 3),
        move(xtab_hbm.at[x_case], xtab, 4),
    ]
    for load in loads:
        load.start()

    def device(dz, dx):
        return (lax.rem(me_z + dz + bricks, bricks), lax.rem(me_x + dx + planes, planes))

    sides = [(dz, dx) for dz in (-1, 0, 1) for dx in (-1, 0, 1) if (dz, dx) != (0, 0)]
    others = [(dz, 0) for dz in range(2, bricks - 1)]
    barrier = pltpu.get_barrier_semaphore()
    for dz, dx in sides + others:
        pl.semaphore_signal(barrier, inc=1, device_id=device(dz, dx), device_id_type=MESH)

    loads[0].wait()
    loads[1].wait()
    body = pl.ds(LANES, cols)
    edges[...] = jnp.dot(
        pick[...], field[0:own, body], preferred_element_type=jnp.float32
    ).astype(jnp.bfloat16)

    pl.semaphore_wait(barrier, len(sides + others))

    z_lo, z_hi = own, own + 2 * xs
    x_lo = own + 4 * xs
    x_hi = x_lo + 2 * zs
    corner = x_hi + 2 * zs
    face = {
        (-1, 0): (dens_hbm.at[0 : 2 * xs], z_hi, 2 * xs),
        (1, 0): (dens_hbm.at[own - 2 * xs : own], z_lo, 2 * xs),
        (0, -1): (edges.at[0 : 2 * zs], x_hi, 2 * zs),
        (0, 1): (edges.at[2 * zs : 4 * zs], x_lo, 2 * zs),
        (-1, -1): (edges.at[4 * zs : 4 * zs + 8], corner + 24, 8),
        (-1, 1): (edges.at[4 * zs + 8 : 4 * zs + 16], corner + 16, 8),
        (1, -1): (edges.at[4 * zs + 16 : 4 * zs + 24], corner + 8, 8),
        (1, 1): (edges.at[4 * zs + 24 : 4 * zs + 32], corner, 8),
    }
    halos = []
    for n, (dz, dx) in enumerate(sides):
        src, row, count = face[dz, dx]
        halos.append(
            pltpu.make_async_remote_copy(
                src_ref=src,
                dst_ref=field.at[row : row + count, body],
                send_sem=halo_send.at[n],
                recv_sem=halo_recv.at[n],
                device_id=device(dz, dx),
                device_id_type=MESH,
            )
        )
    for halo in halos:
        halo.start()

    loads[3].wait()
    loads[4].wait()
    for n in range(len(RESULTS)):
        zc = ztab[n * zs : (n + 1) * zs, :]
        xc = xtab[n * xs : (n + 1) * xs, :]
        block = zc[:, None, :] * xc[None, :, :]
        taps[n * own : (n + 1) * own, :] = block.reshape(own, zc.shape[1]).astype(jnp.bfloat16)

    total_z = zs * bricks
    levels = ext_ref.shape[1]
    lut[...] = jnp.zeros_like(lut)
    lut[0:8, 0:levels] = jnp.broadcast_to(ext_ref[...], (8, levels)) * (
        -2.0 / total_z * float(np.log2(np.e))
    )
    for c in range(3):
        lut[8 * c + 8 : 8 * c + 16, 0:levels] = jnp.broadcast_to(
            color_ref[c : c + 1, :], (8, levels)
        )
    loads[2].wait()

    def look(z, _):
        rows = pl.ds(pl.multiple_of(z * xs, 8), xs)
        for t in range(cols // LANES):
            tile = slice(t * LANES, (t + 1) * LANES)
            index = mats[rows, tile]
            for c in range(4):
                looked[c, rows, tile] = jnp.take_along_axis(
                    lut[8 * c : 8 * c + 8, :], index, axis=1
                )
        return 0

    lax.fori_loop(0, zs, look, 0)

    for halo in halos:
        halo.wait()

    wide = 2 * LANES
    lane_full = lax.broadcasted_iota(jnp.int32, (4 * own, LANES), 1)
    for t in range(cols // wide):
        at = slice(LANES + t * wide, LANES + (t + 1) * wide)
        filtered[:, at] = jnp.dot(taps[...], field[:, at], preferred_element_type=jnp.float32)
    first = filtered[:, LANES : 2 * LANES]
    filtered[:, 0:LANES] = jnp.where(lane_full == LANES - 2, -pltpu.roll(first, LANES - 2, 1), 0.0)
    final = filtered[:, cols : cols + LANES]
    filtered[:, cols + LANES : cols + 2 * LANES] = jnp.where(
        lane_full == 1, -pltpu.roll(final, 2, 1), 0.0
    )

    part = 2 * cols // bricks
    tiles = part // LANES
    span = part + 2 * LANES
    mid = slice(LANES, LANES + part)
    lane = lax.broadcasted_iota(jnp.int32, (xs, LANES), 1)
    low = lane < LANES // 2
    half = LANES // 2

    def partial(dest):
        return pltpu.make_async_remote_copy(
            src_ref=send.at[dest],
            dst_ref=recv.at[me_z],
            send_sem=part_send.at[dest],
            recv_sem=part_recv.at[me_z],
            device_id=(dest, me_x),
            device_id_type=MESH,
        )

    def phase(i, _):
        offset = jnp.where(i == 0, 2, jnp.where(i == 1, 1, jnp.where(i == 2, 3, 0)))
        pair = lax.rem(lax.div(me_z, 2) + offset, bricks // 2)
        start = pl.multiple_of(pair * part, LANES)

        def cells(z, carry):
            clear, red, green, blue = carry
            row = pl.multiple_of(z * xs, 8)

            def near(n):
                u = filtered[pl.ds(row + n * own, xs), pl.ds(start, span)]
                return u

            def shifted(u, by):
                return pltpu.roll(u, by % span, 1)[:, mid]

            u = near(0)
            smooth = shifted(u, 1) + shifted(u, -1) + 2.0 * u[:, mid]
            u = near(1)
            gz = (shifted(u, 2) + shifted(u, -2)) + 4.0 * (shifted(u, 1) + shifted(u, -1)) + 6.0 * u[:, mid]
            u = near(2)
            gx = (shifted(u, 2) + shifted(u, -2)) + 4.0 * (shifted(u, 1) + shifted(u, -1)) + 6.0 * u[:, mid]
            u = near(3)
            gy = (shifted(u, -2) - shifted(u, 2)) + 2.0 * (shifted(u, -1) - shifted(u, 1))
            lit = 0.35 + 0.65 * jnp.abs(LIGHT_Z * gz + LIGHT_X * gx + LIGHT_Y * gy) * lax.rsqrt(
                gz * gz + gx * gx + gy * gy + 1.0
            )
            here = (pl.ds(row, xs), pl.ds(start, part))
            passed = clear * jnp.exp2(looked[(0,) + here] * (smooth * smooth + 0.25))
            weight = (clear - passed) * lit
            return (
                passed,
                red + weight * looked[(1,) + here],
                green + weight * looked[(2,) + here],
                blue + weight * looked[(3,) + here],
            )

        def group(g, carry):
            for k in range(4):
                carry = cells(g * 4 + k, carry)
            return carry

        zero = jnp.zeros((xs, part), jnp.float32)
        clear, red, green, blue = lax.fori_loop(
            0, zs // 4, group, (zero + 1.0, zero, zero, zero)
        )
        fronts = [v[:, 0:LANES] for v in (red, green, blue, clear)]
        mids = [v[:, LANES : 2 * LANES] for v in (red, green, blue, clear)]
        backs = [v[:, 2 * LANES : 3 * LANES] for v in (red, green, blue, clear)]
        swapped = [pltpu.roll(v, half, 1) for v in mids]
        even, odd = 2 * pair, 2 * pair + 1
        for c in range(4):
            send[even, c] = fronts[c]
            send[odd, c] = backs[c]
        for c in range(2):
            send[even, 4 + c] = jnp.where(low, mids[2 * c], swapped[2 * c + 1])
            send[odd, 4 + c] = jnp.where(low, swapped[2 * c], mids[2 * c + 1])
        for dest in (even, odd):

            @pl.when(dest != me_z)
            def _():
                partial(dest).start()

        return 0

    lax.fori_loop(0, bricks // 2, phase, 0)
    recv[me_z] = send[me_z]

    image = [jnp.zeros((xs, LANES), jnp.float32) for _ in range(5)]
    clear = jnp.ones((xs, LANES), jnp.float32)
    clear_half = clear
    for s in range(bricks):

        @pl.when(me_z != s)
        def _():
            pltpu.make_async_remote_copy(
                src_ref=send.at[s],
                dst_ref=recv.at[s],
                send_sem=part_send.at[s],
                recv_sem=part_recv.at[s],
                device_id=(s, me_x),
                device_id_type=MESH,
            ).wait()

        layer = [recv[s, c] for c in range(6)]
        for c in range(3):
            image[c] = image[c] + clear * layer[c]
        image[3] = image[3] + clear_half * layer[4]
        image[4] = image[4] + clear_half * layer[5]
        clear = clear * layer[3]
        clear_half = clear_half * jnp.where(low, pltpu.roll(layer[5], half, 1), layer[5])
    mains = image[0:3] + [1.0 - clear]
    tail = jnp.where(low, image[4], 1.0 - clear_half)
    halves = [image[3], pltpu.roll(image[3], half, 1), tail, pltpu.roll(tail, half, 1)]
    is_even = lax.rem(me_z, 2) == 0
    for c in range(4):
        turned = pltpu.roll(mains[c], half, 1)
        out_ref[c, :, 0:LANES] = jnp.where(is_even, mains[c], jnp.where(low, halves[c], turned))
        out_ref[c, :, LANES : LANES + half] = jnp.where(is_even, halves[c], turned)[:, 0:half]


def shards(density, material, tf_color, tf_extinction):
    bricks = lax.axis_size("depth")
    planes = lax.axis_size("plane")
    zs, xs, cols = density.shape
    own = zs * xs
    ztab, xtab = tables(zs, xs)
    picker = edge_picker(zs, xs)
    gathered = ztab.shape[2]
    hbm = pl.BlockSpec(memory_space=pl.ANY)
    vmem = pl.BlockSpec(memory_space=pltpu.VMEM)
    return pl.pallas_call(
        functools.partial(frame_kernel, zs, xs, cols, bricks, planes),
        out_shape=jax.ShapeDtypeStruct((4, xs, cols // bricks), jnp.float32),
        in_specs=[hbm, hbm, vmem, vmem, hbm, hbm, hbm],
        out_specs=vmem,
        scratch_shapes=[
            pltpu.VMEM((gathered, cols + 2 * LANES), jnp.bfloat16),
            pltpu.VMEM((own, cols), jnp.int32),
            pltpu.VMEM(ztab.shape[1:], jnp.float32),
            pltpu.VMEM(xtab.shape[1:], jnp.float32),
            pltpu.VMEM(picker.shape, jnp.bfloat16),
            pltpu.VMEM((picker.shape[0], cols), jnp.bfloat16),
            pltpu.VMEM((4 * own, gathered), jnp.bfloat16),
            pltpu.VMEM((4 * own, cols + 2 * LANES), jnp.float32),
            pltpu.VMEM((4, own, cols), jnp.float32),
            pltpu.VMEM((32, LANES), jnp.float32),
            pltpu.VMEM((bricks, 6, xs, LANES), jnp.float32),
            pltpu.VMEM((bricks, 6, xs, LANES), jnp.float32),
            pltpu.SemaphoreType.DMA((5,)),
            pltpu.SemaphoreType.DMA((8,)),
            pltpu.SemaphoreType.DMA((8,)),
            pltpu.SemaphoreType.DMA((bricks,)),
            pltpu.SemaphoreType.DMA((bricks,)),
        ],
        compiler_params=pltpu.CompilerParams(collective_id=0, has_side_effects=True),
        name="frame",
    )(
        density.reshape(own, cols),
        material.reshape(own, cols),
        tf_color,
        tf_extinction.reshape(1, -1),
        jnp.asarray(ztab),
        jnp.asarray(xtab),
        jnp.asarray(picker, jnp.bfloat16),
    )


def solution(mesh):
    return jax.shard_map(
        shards,
        mesh=mesh,
        in_specs=(P("depth", "plane", None), P("depth", "plane", None), P(), P()),
        out_specs=P(None, "plane", "depth"),
        check_vma=False,
    )
```

```python
import functools

import jax
import jax.numpy as jnp
import numpy as np
from jax import lax
from jax.experimental import pallas as pl
from jax.experimental.pallas import tpu as pltpu
from jax.sharding import PartitionSpec as P

LIGHT_Z = 0.64
LIGHT_X = 0.48
LIGHT_Y = 0.6
LANES = 128
MESH = pl.DeviceIdType.MESH

TENT = np.array([0.0, 1.0, 2.0, 1.0, 0.0]) / 4.0
TENT_TENT = np.array([1.0, 4.0, 6.0, 4.0, 1.0]) / 16.0
SLOPE_TENT = np.array([-1.0, -2.0, 0.0, 2.0, 1.0]) / 8.0
RESULTS = (
    (TENT, TENT, TENT),
    (SLOPE_TENT, TENT_TENT, TENT_TENT),
    (TENT_TENT, SLOPE_TENT, TENT_TENT),
    (TENT_TENT, TENT_TENT, SLOPE_TENT),
)
SHIFTS = (0, -1, 1, -2, 2)
USED = ((0, 3), (0, 5), (0, 5), (1, 5))


def banded(taps, count, case):
    matrix = np.zeros((count, count + 4))
    for o in range(count):
        matrix[o, o : o + 5] = taps
    if case == 0:
        matrix[:, 2] -= matrix[:, 0]
        matrix[:, 0:2] = 0.0
    if case == 2:
        matrix[:, count + 1] -= matrix[:, count + 3]
        matrix[:, count + 2 : count + 4] = 0.0
    return matrix


def gathered_rows(zs, xs):
    rows = [(z + 2, x + 2) for z in range(zs) for x in range(xs)]
    rows += [(z, x + 2) for z in (0, 1) for x in range(xs)]
    rows += [(zs + 2 + z, x + 2) for z in (0, 1) for x in range(xs)]
    rows += [(z + 2, x) for z in range(zs) for x in (0, 1)]
    rows += [(z + 2, xs + 2 + x) for z in range(zs) for x in (0, 1)]
    for z0 in (0, zs + 2):
        for x0 in (0, xs + 2):
            rows += [(z0 + z, x0 + x) for z in (0, 1) for x in (0, 1)]
            rows += [(-1, -1)] * 4
    return rows


def tables(zs, xs):
    rows = gathered_rows(zs, xs)
    zi = np.array([r[0] for r in rows])
    xi = np.array([r[1] for r in rows])
    keep = (zi >= 0).astype(np.float64)
    zi, xi = np.maximum(zi, 0), np.maximum(xi, 0)
    along_z = [
        np.concatenate([banded(taps[0], zs, case)[:, zi] for taps in RESULTS]) for case in range(3)
    ]
    along_x = [
        np.concatenate([banded(taps[1], xs, case)[:, xi] * keep for taps in RESULTS])
        for case in range(3)
    ]
    return np.stack(along_z).astype(np.float32), np.stack(along_x).astype(np.float32)


def edge_picker(zs, xs):
    own = {(z, x): z * xs + x for z in range(zs) for x in range(xs)}
    wanted = [own[z, x] for z in range(zs) for x in (0, 1)]
    wanted += [own[z, x] for z in range(zs) for x in (xs - 2, xs - 1)]
    for z0 in (0, zs - 2):
        for x0 in (0, xs - 2):
            wanted += [own[z0 + z, x0 + x] for z in (0, 1) for x in (0, 1)]
            wanted += [-1] * 4
    picker = np.zeros((len(wanted), zs * xs), np.float32)
    for row, source in enumerate(wanted):
        if source >= 0:
            picker[row, source] = 1.0
    return picker


def frame_kernel(
    zs, xs, cols, bricks, planes,
    dens_hbm, mat_hbm, color_hbm, ext_hbm, ztab_hbm, xtab_hbm, pick_hbm,
    out_ref,
    field, halo, mats, color, ext, ztab, xtab, pick, edges, corners, corners_in, taps, halo_taps,
    filtered, looked, lut, send, recv,
    load_sem, halo_send, halo_recv, part_send, part_recv,
):
    own = zs * xs
    me_z = lax.axis_index("depth")
    me_x = lax.axis_index("plane")

    def device(dz, dx):
        return (lax.rem(me_z + dz + bricks, bricks), lax.rem(me_x + dx + planes, planes))

    sides = [(-1, -1), (-1, 1), (1, -1), (1, 1), (-1, 0), (1, 0), (0, -1), (0, 1)]
    others = [(dz, 0) for dz in range(2, bricks - 1)]
    barrier = pltpu.get_barrier_semaphore()
    for dz, dx in sides + others:
        pl.semaphore_signal(barrier, inc=1, device_id=device(dz, dx), device_id_type=MESH)

    def move(src, dst, sem):
        return pltpu.make_async_copy(src, dst, load_sem.at[sem])

    z_case = jnp.where(me_z == 0, 0, jnp.where(me_z == bricks - 1, 2, 1))
    x_case = jnp.where(me_x == 0, 0, jnp.where(me_x == planes - 1, 2, 1))
    loads = [
        move(dens_hbm, field.at[0:own], 0),
        move(pick_hbm, pick, 1),
        move(ztab_hbm.at[z_case], ztab, 2),
        move(xtab_hbm.at[x_case], xtab, 3),
        move(color_hbm, color, 4),
        move(ext_hbm, ext, 5),
        move(mat_hbm, mats, 6),
    ]
    for load in loads:
        load.start()

    loads[0].wait()
    loads[1].wait()
    picked = jnp.dot(
        pick[...], field[0:own, :], preferred_element_type=jnp.float32
    ).astype(jnp.bfloat16)
    edges[...] = picked[0 : 4 * zs]
    for n in range(4):
        corners[n] = picked[4 * zs + 8 * n : 4 * zs + 8 * n + 4]

    pl.semaphore_wait(barrier, len(sides + others))

    z_lo, z_hi = 0, 2 * xs
    x_lo = 4 * xs
    x_hi = x_lo + 2 * zs
    corner = x_hi + 2 * zs
    gathered = corner + 32
    face = {
        (-1, 0): (dens_hbm.at[0 : 2 * xs], halo.at[z_hi : z_hi + 2 * xs]),
        (1, 0): (dens_hbm.at[own - 2 * xs : own], halo.at[z_lo : z_lo + 2 * xs]),
        (0, -1): (edges.at[0 : 2 * zs], halo.at[x_hi : x_hi + 2 * zs]),
        (0, 1): (edges.at[2 * zs : 4 * zs], halo.at[x_lo : x_lo + 2 * zs]),
        (-1, -1): (corners.at[0], corners_in.at[3]),
        (-1, 1): (corners.at[1], corners_in.at[2]),
        (1, -1): (corners.at[2], corners_in.at[1]),
        (1, 1): (corners.at[3], corners_in.at[0]),
    }
    halos = []
    for n, (dz, dx) in enumerate(sides):
        src, dst = face[dz, dx]
        halos.append(
            pltpu.make_async_remote_copy(
                src_ref=src,
                dst_ref=dst,
                send_sem=halo_send.at[n],
                recv_sem=halo_recv.at[n],
                device_id=device(dz, dx),
                device_id_type=MESH,
            )
        )
    for transfer in halos:
        transfer.start()

    loads[2].wait()
    loads[3].wait()
    for n, (_, _, y_taps) in enumerate(RESULTS):
        zc = ztab[n * zs : (n + 1) * zs, :]
        xc = xtab[n * xs : (n + 1) * xs, :]
        block = (zc[:, None, :] * xc[None, :, :]).reshape(own, own + gathered)
        rows = slice(n * own, (n + 1) * own)
        for k in range(*USED[n]):
            scaled = (block * float(y_taps[SHIFTS[k] + 2])).astype(jnp.bfloat16)
            taps[rows, k * own : (k + 1) * own] = scaled[:, 0:own]
            halo_taps[rows, k * gathered : (k + 1) * gathered] = scaled[:, own:]

    def spread(ref, count):
        for r in range(0, count, 16):
            rows = ref[r : r + 16, :]
            first, final = rows[:, 0:LANES], rows[:, cols - LANES : cols]
            at = lax.broadcasted_iota(jnp.int32, first.shape, 1)
            for k, shift in enumerate(SHIFTS):
                if shift == 0:
                    continue
                to = slice(k * count + r, k * count + r + 16)
                moved = pltpu.roll(rows, -shift % cols, 1)
                ref[to, :] = moved
                nothing = jnp.zeros_like(first)
                if shift < 0:
                    edge = jnp.where(at == -shift - 1, nothing, moved[:, 0:LANES])
                    if shift == -2:
                        edge = jnp.where(at == 0, -first, edge)
                    ref[to, 0:LANES] = edge
                else:
                    edge = jnp.where(at == LANES - shift, nothing, moved[:, cols - LANES : cols])
                    if shift == 2:
                        edge = jnp.where(at == LANES - 1, -final, edge)
                    ref[to, cols - LANES : cols] = edge

    def contract(coefficients, ref, count, n, at):
        lo, hi = USED[n]
        return jnp.dot(
            coefficients[n * own : (n + 1) * own, lo * count : hi * count],
            ref[lo * count : hi * count, at],
            preferred_element_type=jnp.float32,
        )

    wide = 2 * LANES
    spread(field, own)
    for t in range(cols // wide):
        at = slice(t * wide, (t + 1) * wide)
        for n in range(4):
            filtered[n * own : (n + 1) * own, at] = contract(taps, field, own, n, at)

    total_z = zs * bricks
    for n in (4, 5, 6):
        loads[n].wait()
    levels = ext.shape[1]
    lut[...] = jnp.zeros_like(lut)
    lut[0:8, 0:levels] = jnp.broadcast_to(ext[...], (8, levels)) * (
        -2.0 / total_z * float(np.log2(np.e))
    )
    for c in range(3):
        lut[8 * c + 8 : 8 * c + 16, 0:levels] = jnp.broadcast_to(color[c : c + 1, :], (8, levels))

    def look(z, _):
        rows = pl.ds(pl.multiple_of(z * xs, 8), xs)
        for t in range(cols // LANES):
            tile = slice(t * LANES, (t + 1) * LANES)
            index = mats[rows, tile]
            for c in range(4):
                looked[c, rows, tile] = jnp.take_along_axis(
                    lut[8 * c : 8 * c + 8, :], index, axis=1
                )
        return 0

    lax.fori_loop(0, zs, look, 0)

    for transfer in halos:
        transfer.wait()

    for n in range(4):
        halo[corner + 8 * n : corner + 8 * n + 8, :] = jnp.concatenate(
            [corners_in[n], jnp.zeros_like(corners_in[n])], axis=0
        )
    spread(halo, gathered)
    for t in range(cols // wide):
        at = slice(t * wide, (t + 1) * wide)
        for n in range(4):
            rows = slice(n * own, (n + 1) * own)
            filtered[rows, at] = filtered[rows, at] + contract(halo_taps, halo, gathered, n, at)

    part = 2 * cols // bricks
    lane = lax.broadcasted_iota(jnp.int32, (xs, LANES), 1)
    low = lane < LANES // 2
    half = LANES // 2

    def partial(dest):
        return pltpu.make_async_remote_copy(
            src_ref=send.at[dest],
            dst_ref=recv.at[me_z],
            send_sem=part_send.at[dest],
            recv_sem=part_recv.at[me_z],
            device_id=(dest, me_x),
            device_id_type=MESH,
        )

    def phase(i, _):
        offset = jnp.where(i == 0, 2, jnp.where(i == 1, 1, jnp.where(i == 2, 3, 0)))
        pair = lax.rem(lax.div(me_z, 2) + offset, bricks // 2)
        start = pl.multiple_of(pair * part, LANES)

        def cells(z, carry):
            clear, red, green, blue = carry
            row = pl.multiple_of(z * xs, 8)

            here = (pl.ds(row, xs), pl.ds(start, part))
            smooth, gz, gx, gy = [
                filtered[pl.ds(row + n * own, xs), pl.ds(start, part)] for n in range(4)
            ]
            lit = 0.35 + 0.65 * jnp.abs(LIGHT_Z * gz + LIGHT_X * gx + LIGHT_Y * gy) * lax.rsqrt(
                gz * gz + gx * gx + gy * gy + 1.0
            )
            passed = clear * jnp.exp2(looked[(0,) + here] * (smooth * smooth + 0.25))
            weight = (clear - passed) * lit
            return (
                passed,
                red + weight * looked[(1,) + here],
                green + weight * looked[(2,) + here],
                blue + weight * looked[(3,) + here],
            )

        def group(g, carry):
            for k in range(4):
                carry = cells(g * 4 + k, carry)
            return carry

        zero = jnp.zeros((xs, part), jnp.float32)
        clear, red, green, blue = lax.fori_loop(
            0, zs // 4, group, (zero + 1.0, zero, zero, zero)
        )
        fronts = [v[:, 0:LANES] for v in (red, green, blue, clear)]
        mids = [v[:, LANES : 2 * LANES] for v in (red, green, blue, clear)]
        backs = [v[:, 2 * LANES : 3 * LANES] for v in (red, green, blue, clear)]
        swapped = [pltpu.roll(v, half, 1) for v in mids]
        even, odd = 2 * pair, 2 * pair + 1
        for c in range(4):
            send[even, c] = fronts[c]
            send[odd, c] = backs[c]
        for c in range(2):
            send[even, 4 + c] = jnp.where(low, mids[2 * c], swapped[2 * c + 1])
            send[odd, 4 + c] = jnp.where(low, swapped[2 * c], mids[2 * c + 1])
        for dest in (even, odd):

            @pl.when(dest != me_z)
            def _():
                partial(dest).start()

        return 0

    lax.fori_loop(0, bricks // 2, phase, 0)
    recv[me_z] = send[me_z]

    image = [jnp.zeros((xs, LANES), jnp.float32) for _ in range(5)]
    clear = jnp.ones((xs, LANES), jnp.float32)
    clear_half = clear
    for s in range(bricks):

        @pl.when(me_z != s)
        def _():
            pltpu.make_async_remote_copy(
                src_ref=send.at[s],
                dst_ref=recv.at[s],
                send_sem=part_send.at[s],
                recv_sem=part_recv.at[s],
                device_id=(s, me_x),
                device_id_type=MESH,
            ).wait()

        layer = [recv[s, c] for c in range(6)]
        for c in range(3):
            image[c] = image[c] + clear * layer[c]
        image[3] = image[3] + clear_half * layer[4]
        image[4] = image[4] + clear_half * layer[5]
        clear = clear * layer[3]
        clear_half = clear_half * jnp.where(low, pltpu.roll(layer[5], half, 1), layer[5])
    mains = image[0:3] + [1.0 - clear]
    tail = jnp.where(low, image[4], 1.0 - clear_half)
    halves = [image[3], pltpu.roll(image[3], half, 1), tail, pltpu.roll(tail, half, 1)]
    is_even = lax.rem(me_z, 2) == 0
    for c in range(4):
        turned = pltpu.roll(mains[c], half, 1)
        out_ref[c, :, 0:LANES] = jnp.where(is_even, mains[c], jnp.where(low, halves[c], turned))
        out_ref[c, :, LANES : LANES + half] = jnp.where(is_even, halves[c], turned)[:, 0:half]


def shards(density, material, tf_color, tf_extinction):
    bricks = lax.axis_size("depth")
    planes = lax.axis_size("plane")
    zs, xs, cols = density.shape
    own = zs * xs
    ztab, xtab = tables(zs, xs)
    picker = edge_picker(zs, xs)
    gathered = ztab.shape[2] - own
    hbm = pl.BlockSpec(memory_space=pl.ANY)
    vmem = pl.BlockSpec(memory_space=pltpu.VMEM)
    shifts = len(SHIFTS)
    return pl.pallas_call(
        functools.partial(frame_kernel, zs, xs, cols, bricks, planes),
        out_shape=jax.ShapeDtypeStruct((4, xs, cols // bricks), jnp.float32),
        in_specs=[hbm] * 7,
        out_specs=vmem,
        scratch_shapes=[
            pltpu.VMEM((shifts * own, cols), jnp.bfloat16),
            pltpu.VMEM((shifts * gathered, cols), jnp.bfloat16),
            pltpu.VMEM((own, cols), jnp.int32),
            pltpu.VMEM(tf_color.shape, jnp.float32),
            pltpu.VMEM((1, tf_extinction.shape[0]), jnp.float32),
            pltpu.VMEM(ztab.shape[1:], jnp.float32),
            pltpu.VMEM(xtab.shape[1:], jnp.float32),
            pltpu.VMEM(picker.shape, jnp.bfloat16),
            pltpu.VMEM((4 * zs, cols), jnp.bfloat16),
            pltpu.VMEM((4, 4, cols), jnp.bfloat16),
            pltpu.VMEM((4, 4, cols), jnp.bfloat16),
            pltpu.VMEM((4 * own, shifts * own), jnp.bfloat16),
            pltpu.VMEM((4 * own, shifts * gathered), jnp.bfloat16),
            pltpu.VMEM((4 * own, cols), jnp.float32),
            pltpu.VMEM((4, own, cols), jnp.float32),
            pltpu.VMEM((32, LANES), jnp.float32),
            pltpu.VMEM((bricks, 6, xs, LANES), jnp.float32),
            pltpu.VMEM((bricks, 6, xs, LANES), jnp.float32),
            pltpu.SemaphoreType.DMA((7,)),
            pltpu.SemaphoreType.DMA((8,)),
            pltpu.SemaphoreType.DMA((8,)),
            pltpu.SemaphoreType.DMA((bricks,)),
            pltpu.SemaphoreType.DMA((bricks,)),
        ],
        compiler_params=pltpu.CompilerParams(collective_id=0, has_side_effects=True),
        name="frame",
    )(
        density.reshape(own, cols),
        material.reshape(own, cols),
        tf_color,
        tf_extinction.reshape(1, -1),
        jnp.asarray(ztab),
        jnp.asarray(xtab),
        jnp.asarray(picker, jnp.bfloat16),
    )


def solution(mesh):
    return jax.shard_map(
        shards,
        mesh=mesh,
        in_specs=(P("depth", "plane", None), P("depth", "plane", None), P(), P()),
        out_specs=P(None, "plane", "depth"),
        check_vma=False,
    )
```

```python
import functools

import jax
import jax.numpy as jnp
import numpy as np
from jax import lax
from jax.experimental import pallas as pl
from jax.experimental.pallas import tpu as pltpu
from jax.sharding import PartitionSpec as P

LIGHT_Z = 0.64
LIGHT_X = 0.48
LIGHT_Y = 0.6
LANES = 128
MESH = pl.DeviceIdType.MESH

TENT = np.array([0.0, 1.0, 2.0, 1.0, 0.0]) / 4.0
TENT_TENT = np.array([1.0, 4.0, 6.0, 4.0, 1.0]) / 16.0
SLOPE_TENT = np.array([-1.0, -2.0, 0.0, 2.0, 1.0]) / 8.0
RESULTS = (
    (TENT, TENT, TENT),
    (SLOPE_TENT, TENT_TENT, TENT_TENT),
    (TENT_TENT, SLOPE_TENT, TENT_TENT),
    (TENT_TENT, TENT_TENT, SLOPE_TENT),
)
SHIFTS = (0, -1, 1, -2, 2)


def banded(taps, count, case):
    matrix = np.zeros((count, count + 4))
    for o in range(count):
        matrix[o, o : o + 5] = taps
    if case == 0:
        matrix[:, 2] -= matrix[:, 0]
        matrix[:, 0:2] = 0.0
    if case == 2:
        matrix[:, count + 1] -= matrix[:, count + 3]
        matrix[:, count + 2 : count + 4] = 0.0
    return matrix


def gathered_rows(zs, xs):
    rows = [(z + 2, x + 2) for z in range(zs) for x in range(xs)]
    rows += [(z, x + 2) for z in (0, 1) for x in range(xs)]
    rows += [(zs + 2 + z, x + 2) for z in (0, 1) for x in range(xs)]
    rows += [(z + 2, x) for z in range(zs) for x in (0, 1)]
    rows += [(z + 2, xs + 2 + x) for z in range(zs) for x in (0, 1)]
    for z0 in (0, zs + 2):
        for x0 in (0, xs + 2):
            rows += [(z0 + z, x0 + x) for z in (0, 1) for x in (0, 1)]
            rows += [(-1, -1)] * 4
    return rows


def tables(zs, xs):
    rows = gathered_rows(zs, xs)
    zi = np.array([r[0] for r in rows])
    xi = np.array([r[1] for r in rows])
    keep = (zi >= 0).astype(np.float64)
    zi, xi = np.maximum(zi, 0), np.maximum(xi, 0)
    along_z = [
        np.concatenate([banded(taps[0], zs, case)[:, zi] for taps in RESULTS]) for case in range(3)
    ]
    along_x = [
        np.concatenate([banded(taps[1], xs, case)[:, xi] * keep for taps in RESULTS])
        for case in range(3)
    ]
    return np.stack(along_z).astype(np.float32), np.stack(along_x).astype(np.float32)


def edge_picker(zs, xs):
    own = {(z, x): z * xs + x for z in range(zs) for x in range(xs)}
    wanted = [own[z, x] for z in range(zs) for x in (0, 1)]
    wanted += [own[z, x] for z in range(zs) for x in (xs - 2, xs - 1)]
    for z0 in (0, zs - 2):
        for x0 in (0, xs - 2):
            wanted += [own[z0 + z, x0 + x] for z in (0, 1) for x in (0, 1)]
            wanted += [-1] * 4
    picker = np.zeros((len(wanted), zs * xs), np.float32)
    for row, source in enumerate(wanted):
        if source >= 0:
            picker[row, source] = 1.0
    return picker


def frame_kernel(
    zs, xs, cols, bricks, planes,
    dens_hbm, mat_hbm, color_hbm, ext_hbm, ztab_hbm, xtab_hbm, pick_hbm,
    out_ref,
    field, halo, mats, color, ext, ztab, xtab, pick, edges, corners, corners_in, taps, halo_taps,
    filtered, chunk, looked, lut, send, recv,
    load_sem, halo_send, halo_recv, part_send, part_recv,
):
    own = zs * xs
    me_z = lax.axis_index("depth")
    me_x = lax.axis_index("plane")

    def device(dz, dx):
        return (lax.rem(me_z + dz + bricks, bricks), lax.rem(me_x + dx + planes, planes))

    sides = [(-1, -1), (-1, 1), (1, -1), (1, 1), (-1, 0), (1, 0), (0, -1), (0, 1)]
    others = [(dz, 0) for dz in range(2, bricks - 1)]
    barrier = pltpu.get_barrier_semaphore()
    for dz, dx in sides + others:
        pl.semaphore_signal(barrier, inc=1, device_id=device(dz, dx), device_id_type=MESH)

    def move(src, dst, sem):
        return pltpu.make_async_copy(src, dst, load_sem.at[sem])

    z_case = jnp.where(me_z == 0, 0, jnp.where(me_z == bricks - 1, 2, 1))
    x_case = jnp.where(me_x == 0, 0, jnp.where(me_x == planes - 1, 2, 1))
    loads = [
        move(dens_hbm, field.at[0:own], 0),
        move(pick_hbm, pick, 1),
        move(ztab_hbm.at[z_case], ztab, 2),
        move(xtab_hbm.at[x_case], xtab, 3),
        move(color_hbm, color, 4),
        move(ext_hbm, ext, 5),
        move(mat_hbm, mats, 6),
    ]
    for load in loads:
        load.start()

    loads[0].wait()
    loads[1].wait()
    picked = jnp.dot(
        pick[...], field[0:own, :], preferred_element_type=jnp.float32
    ).astype(jnp.bfloat16)
    edges[...] = picked[0 : 4 * zs]
    for n in range(4):
        corners[n] = picked[4 * zs + 8 * n : 4 * zs + 8 * n + 4]

    pl.semaphore_wait(barrier, len(sides + others))

    z_lo, z_hi = 0, 2 * xs
    x_lo = 4 * xs
    x_hi = x_lo + 2 * zs
    corner = x_hi + 2 * zs
    gathered = corner + 32
    face = {
        (-1, 0): (dens_hbm.at[0 : 2 * xs], halo.at[z_hi : z_hi + 2 * xs]),
        (1, 0): (dens_hbm.at[own - 2 * xs : own], halo.at[z_lo : z_lo + 2 * xs]),
        (0, -1): (edges.at[0 : 2 * zs], halo.at[x_hi : x_hi + 2 * zs]),
        (0, 1): (edges.at[2 * zs : 4 * zs], halo.at[x_lo : x_lo + 2 * zs]),
        (-1, -1): (corners.at[0], corners_in.at[3]),
        (-1, 1): (corners.at[1], corners_in.at[2]),
        (1, -1): (corners.at[2], corners_in.at[1]),
        (1, 1): (corners.at[3], corners_in.at[0]),
    }
    halos = []
    for n, (dz, dx) in enumerate(sides):
        src, dst = face[dz, dx]
        halos.append(
            pltpu.make_async_remote_copy(
                src_ref=src,
                dst_ref=dst,
                send_sem=halo_send.at[n],
                recv_sem=halo_recv.at[n],
                device_id=device(dz, dx),
                device_id_type=MESH,
            )
        )
    for transfer in halos:
        transfer.start()

    loads[2].wait()
    loads[3].wait()
    for n, (_, _, y_taps) in enumerate(RESULTS):
        zc = ztab[n * zs : (n + 1) * zs, :]
        xc = xtab[n * xs : (n + 1) * xs, :]
        block = (zc[:, None, :] * xc[None, :, :]).reshape(own, own + gathered)
        rows = slice(n * own, (n + 1) * own)
        for k in range(len(SHIFTS)):
            scaled = (block * float(y_taps[SHIFTS[k] + 2])).astype(jnp.bfloat16)
            taps[rows, k * own : (k + 1) * own] = scaled[:, 0:own]
            halo_taps[rows, k * gathered : (k + 1) * gathered] = scaled[:, own:]

    def spread(ref, count, lo, hi):
        left, right = max(lo - LANES, 0), min(hi + LANES, cols)
        for r in range(0, count, 16):
            rows = ref[r : r + 16, left:right]
            first, final = rows[:, 0:LANES], rows[:, right - left - LANES :]
            nothing = jnp.zeros_like(first)
            at = lax.broadcasted_iota(jnp.int32, first.shape, 1)
            for k, shift in enumerate(SHIFTS):
                if shift == 0:
                    continue
                to = slice(k * count + r, k * count + r + 16)
                moved = pltpu.roll(rows, -shift % (right - left), 1)[:, lo - left : hi - left]
                ref[to, lo:hi] = moved
                if shift < 0 and lo == 0:
                    edge = jnp.where(at == -shift - 1, nothing, moved[:, 0:LANES])
                    if shift == -2:
                        edge = jnp.where(at == 0, -first, edge)
                    ref[to, 0:LANES] = edge
                if shift > 0 and hi == cols:
                    edge = jnp.where(at == LANES - shift, nothing, moved[:, hi - lo - LANES :])
                    if shift == 2:
                        edge = jnp.where(at == LANES - 1, -final, edge)
                    ref[to, cols - LANES : cols] = edge

    wide = 2 * LANES
    spread(field, own, 0, cols)
    for t in range(cols // wide):
        at = slice(t * wide, (t + 1) * wide)
        filtered[:, at] = jnp.dot(taps[...], field[:, at], preferred_element_type=jnp.float32)

    total_z = zs * bricks
    for n in (4, 5, 6):
        loads[n].wait()
    levels = ext.shape[1]
    lut[...] = jnp.zeros_like(lut)
    lut[0:8, 0:levels] = jnp.broadcast_to(ext[...], (8, levels)) * (
        -2.0 / total_z * float(np.log2(np.e))
    )
    for c in range(3):
        lut[8 * c + 8 : 8 * c + 16, 0:levels] = jnp.broadcast_to(color[c : c + 1, :], (8, levels))

    def look(z, _):
        rows = pl.ds(pl.multiple_of(z * xs, 8), xs)
        for t in range(cols // LANES):
            tile = slice(t * LANES, (t + 1) * LANES)
            index = mats[rows, tile]
            for c in range(4):
                looked[c, rows, tile] = jnp.take_along_axis(
                    lut[8 * c : 8 * c + 8, :], index, axis=1
                )
        return 0

    lax.fori_loop(0, zs, look, 0)

    for transfer in halos:
        transfer.wait()

    for n in range(4):
        halo[corner + 8 * n : corner + 8 * n + 8, :] = jnp.concatenate(
            [corners_in[n], jnp.zeros_like(corners_in[n])], axis=0
        )

    part = 2 * cols // bricks
    lane = lax.broadcasted_iota(jnp.int32, (xs, LANES), 1)
    low = lane < LANES // 2
    half = LANES // 2

    def encode(values):
        roots = jnp.sqrt(jnp.clip(jnp.concatenate(values, axis=0), 0.0, 1.0))
        return (jnp.round(roots * 65535.0) - 32768.0).astype(jnp.int32).astype(jnp.int16)

    def decode(code):
        roots = (code.astype(jnp.int32).astype(jnp.float32) + 32768.0) * (1.0 / 65535.0)
        return roots * roots

    def partial(dest):
        return pltpu.make_async_remote_copy(
            src_ref=send.at[dest],
            dst_ref=recv.at[me_z],
            send_sem=part_send.at[dest],
            recv_sem=part_recv.at[me_z],
            device_id=(dest, me_x),
            device_id_type=MESH,
        )

    pairs = bricks // 2
    mine = lax.div(me_z, 2)

    def pair_at(i):
        pair = 0
        for q in range(pairs):
            far = sorted(range(pairs), key=lambda p: (p != 0, -min((p - q) % pairs, (q - p) % pairs)))
            for k, p in enumerate(far):
                pair = jnp.where((mine == q) & (i == k), p, pair)
        return pair

    def render(pair):
        start = pl.multiple_of(pair * part, LANES) if not isinstance(pair, int) else pair * part
        at = pl.ds(start, part)
        chunk[...] = filtered[:, at] + jnp.dot(
            halo_taps[...], halo[:, at], preferred_element_type=jnp.float32
        )

        def cells(z, carry):
            clear, red, green, blue = carry
            row = pl.multiple_of(z * xs, 8)

            here = (pl.ds(row, xs), pl.ds(start, part))
            smooth, gz, gx, gy = [chunk[pl.ds(row + n * own, xs), :] for n in range(4)]
            lit = 0.35 + 0.65 * jnp.abs(LIGHT_Z * gz + LIGHT_X * gx + LIGHT_Y * gy) * lax.rsqrt(
                gz * gz + gx * gx + gy * gy + 1.0
            )
            passed = clear * jnp.exp2(looked[(0,) + here] * (smooth * smooth + 0.25))
            weight = (clear - passed) * lit
            return (
                passed,
                red + weight * looked[(1,) + here],
                green + weight * looked[(2,) + here],
                blue + weight * looked[(3,) + here],
            )

        def group(g, carry):
            for k in range(4):
                carry = cells(g * 4 + k, carry)
            return carry

        zero = jnp.zeros((xs, part), jnp.float32)
        clear, red, green, blue = lax.fori_loop(
            0, zs // 4, group, (zero + 1.0, zero, zero, zero)
        )
        result = (red, green, blue, 1.0 - clear)
        fronts = [v[:, 0:LANES] for v in result]
        mids = [v[:, LANES : 2 * LANES] for v in result]
        backs = [v[:, 2 * LANES : 3 * LANES] for v in result]
        swapped = [pltpu.roll(v, half, 1) for v in mids]
        even, odd = 2 * pair, 2 * pair + 1
        send[even] = encode(
            fronts + [jnp.where(low, mids[2 * c], swapped[2 * c + 1]) for c in (0, 1)]
        )
        send[odd] = encode(
            backs + [jnp.where(low, swapped[2 * c], mids[2 * c + 1]) for c in (0, 1)]
        )
        for dest in (even, odd):

            @pl.when(dest != me_z)
            def _():
                partial(dest).start()

        return 0

    spread(halo, gathered, 0, part)
    render(0)
    spread(halo, gathered, part, cols)
    lax.fori_loop(1, pairs, lambda i, _: render(pair_at(i)), 0)
    recv[me_z] = send[me_z]

    image = [jnp.zeros((xs, LANES), jnp.float32) for _ in range(5)]
    clear = jnp.ones((xs, LANES), jnp.float32)
    clear_half = clear
    for s in range(bricks):

        @pl.when(me_z != s)
        def _():
            pltpu.make_async_remote_copy(
                src_ref=send.at[s],
                dst_ref=recv.at[s],
                send_sem=part_send.at[s],
                recv_sem=part_recv.at[s],
                device_id=(s, me_x),
                device_id_type=MESH,
            ).wait()

        values = decode(recv[s])
        layer = [values[c * xs : (c + 1) * xs] for c in range(6)]
        for c in range(3):
            image[c] = image[c] + clear * layer[c]
        image[3] = image[3] + clear_half * layer[4]
        image[4] = image[4] + clear_half * layer[5]
        clear = clear * (1.0 - layer[3])
        clear_half = clear_half * (1.0 - jnp.where(low, pltpu.roll(layer[5], half, 1), layer[5]))
    mains = image[0:3] + [1.0 - clear]
    tail = jnp.where(low, image[4], 1.0 - clear_half)
    halves = [image[3], pltpu.roll(image[3], half, 1), tail, pltpu.roll(tail, half, 1)]
    is_even = lax.rem(me_z, 2) == 0
    for c in range(4):
        turned = pltpu.roll(mains[c], half, 1)
        out_ref[c, :, 0:LANES] = jnp.where(is_even, mains[c], jnp.where(low, halves[c], turned))
        out_ref[c, :, LANES : LANES + half] = jnp.where(is_even, halves[c], turned)[:, 0:half]


def shards(density, material, tf_color, tf_extinction):
    bricks = lax.axis_size("depth")
    planes = lax.axis_size("plane")
    zs, xs, cols = density.shape
    own = zs * xs
    ztab, xtab = tables(zs, xs)
    picker = edge_picker(zs, xs)
    gathered = ztab.shape[2] - own
    hbm = pl.BlockSpec(memory_space=pl.ANY)
    vmem = pl.BlockSpec(memory_space=pltpu.VMEM)
    shifts = len(SHIFTS)
    return pl.pallas_call(
        functools.partial(frame_kernel, zs, xs, cols, bricks, planes),
        out_shape=pltpu.VMEM((4, xs, cols // bricks), jnp.float32),
        in_specs=[hbm] * 7,
        out_specs=vmem,
        scratch_shapes=[
            pltpu.VMEM((shifts * own, cols), jnp.bfloat16),
            pltpu.VMEM((shifts * gathered, cols), jnp.bfloat16),
            pltpu.VMEM((own, cols), jnp.int32),
            pltpu.VMEM(tf_color.shape, jnp.float32),
            pltpu.VMEM((1, tf_extinction.shape[0]), jnp.float32),
            pltpu.VMEM(ztab.shape[1:], jnp.float32),
            pltpu.VMEM(xtab.shape[1:], jnp.float32),
            pltpu.VMEM(picker.shape, jnp.bfloat16),
            pltpu.VMEM((4 * zs, cols), jnp.bfloat16),
            pltpu.VMEM((4, 4, cols), jnp.bfloat16),
            pltpu.VMEM((4, 4, cols), jnp.bfloat16),
            pltpu.VMEM((4 * own, shifts * own), jnp.bfloat16),
            pltpu.VMEM((4 * own, shifts * gathered), jnp.bfloat16),
            pltpu.VMEM((4 * own, cols), jnp.float32),
            pltpu.VMEM((4 * own, 2 * cols // bricks), jnp.float32),
            pltpu.VMEM((4, own, cols), jnp.float32),
            pltpu.VMEM((32, LANES), jnp.float32),
            pltpu.VMEM((bricks, 6 * xs, LANES), jnp.int16),
            pltpu.VMEM((bricks, 6 * xs, LANES), jnp.int16),
            pltpu.SemaphoreType.DMA((7,)),
            pltpu.SemaphoreType.DMA((8,)),
            pltpu.SemaphoreType.DMA((8,)),
            pltpu.SemaphoreType.DMA((bricks,)),
            pltpu.SemaphoreType.DMA((bricks,)),
        ],
        compiler_params=pltpu.CompilerParams(collective_id=0, has_side_effects=True),
        name="frame",
    )(
        density.reshape(own, cols),
        material.reshape(own, cols),
        tf_color,
        tf_extinction.reshape(1, -1),
        jnp.asarray(ztab),
        jnp.asarray(xtab),
        jnp.asarray(picker, jnp.bfloat16),
    )


def solution(mesh):
    return jax.shard_map(
        shards,
        mesh=mesh,
        in_specs=(P("depth", "plane", None), P("depth", "plane", None), P(), P()),
        out_specs=P(None, "plane", "depth"),
        check_vma=False,
    )
```

```python
import functools

import jax
import jax.numpy as jnp
import numpy as np
from jax import lax
from jax.experimental import pallas as pl
from jax.experimental.pallas import tpu as pltpu
from jax.sharding import PartitionSpec as P

LIGHT_Z = 0.64
LIGHT_X = 0.48
LIGHT_Y = 0.6
LANES = 128
MESH = pl.DeviceIdType.MESH

TENT = np.array([0.0, 1.0, 2.0, 1.0, 0.0]) / 4.0
TENT_TENT = np.array([1.0, 4.0, 6.0, 4.0, 1.0]) / 16.0
SLOPE_TENT = np.array([-1.0, -2.0, 0.0, 2.0, 1.0]) / 8.0
RESULTS = (
    (TENT, TENT, TENT),
    (SLOPE_TENT, TENT_TENT, TENT_TENT),
    (TENT_TENT, SLOPE_TENT, TENT_TENT),
    (TENT_TENT, TENT_TENT, SLOPE_TENT),
)
SHIFTS = (0, -1, 1, -2, 2)


def banded(taps, count, case):
    matrix = np.zeros((count, count + 4))
    for o in range(count):
        matrix[o, o : o + 5] = taps
    if case == 0:
        matrix[:, 2] -= matrix[:, 0]
        matrix[:, 0:2] = 0.0
    if case == 2:
        matrix[:, count + 1] -= matrix[:, count + 3]
        matrix[:, count + 2 : count + 4] = 0.0
    return matrix


def gathered_rows(zs, xs):
    rows = [(z + 2, x + 2) for z in range(zs) for x in range(xs)]
    rows += [(z, x + 2) for z in (0, 1) for x in range(xs)]
    rows += [(zs + 2 + z, x + 2) for z in (0, 1) for x in range(xs)]
    rows += [(z + 2, x) for z in range(zs) for x in (0, 1)]
    rows += [(z + 2, xs + 2 + x) for z in range(zs) for x in (0, 1)]
    for z0 in (0, zs + 2):
        for x0 in (0, xs + 2):
            rows += [(z0 + z, x0 + x) for z in (0, 1) for x in (0, 1)]
            rows += [(-1, -1)] * 4
    return rows


def tables(zs, xs):
    rows = gathered_rows(zs, xs)
    zi = np.array([r[0] for r in rows])
    xi = np.array([r[1] for r in rows])
    keep = (zi >= 0).astype(np.float64)
    zi, xi = np.maximum(zi, 0), np.maximum(xi, 0)
    along_z = [
        np.concatenate([banded(taps[0], zs, case)[:, zi] for taps in RESULTS]) for case in range(3)
    ]
    along_x = [
        np.concatenate([banded(taps[1], xs, case)[:, xi] * keep for taps in RESULTS])
        for case in range(3)
    ]
    return np.stack(along_z).astype(np.float32), np.stack(along_x).astype(np.float32)


def edge_picker(zs, xs):
    own = {(z, x): z * xs + x for z in range(zs) for x in range(xs)}
    wanted = [own[z, x] for z in range(zs) for x in (0, 1)]
    wanted += [own[z, x] for z in range(zs) for x in (xs - 2, xs - 1)]
    for z0 in (0, zs - 2):
        for x0 in (0, xs - 2):
            wanted += [own[z0 + z, x0 + x] for z in (0, 1) for x in (0, 1)]
            wanted += [-1] * 4
    picker = np.zeros((len(wanted), zs * xs), np.float32)
    for row, source in enumerate(wanted):
        if source >= 0:
            picker[row, source] = 1.0
    return picker


def frame_kernel(
    zs, xs, cols, bricks, planes,
    dens_hbm, mat_hbm, color_hbm, ext_hbm, ztab_hbm, xtab_hbm, pick_hbm,
    out_ref,
    field, halo, mats, color, ext, ztab, xtab, pick, edges, corners, corners_in, taps, halo_taps,
    filtered, chunk, looked, lut, send, recv,
    load_sem, ready, halo_send, halo_recv, part_send, part_recv,
):
    own = zs * xs
    me_z = lax.axis_index("depth")
    me_x = lax.axis_index("plane")

    def device(dz, dx):
        return (lax.rem(me_z + dz + bricks, bricks), lax.rem(me_x + dx + planes, planes))

    sides = [(-1, -1), (-1, 1), (1, -1), (1, 1), (-1, 0), (1, 0), (0, -1), (0, 1)]
    barrier = pltpu.get_barrier_semaphore()
    for dz, dx in sides:
        pl.semaphore_signal(barrier, inc=1, device_id=device(dz, dx), device_id_type=MESH)

    def move(src, dst, sem):
        return pltpu.make_async_copy(src, dst, load_sem.at[sem])

    z_case = jnp.where(me_z == 0, 0, jnp.where(me_z == bricks - 1, 2, 1))
    x_case = jnp.where(me_x == 0, 0, jnp.where(me_x == planes - 1, 2, 1))
    loads = [
        move(dens_hbm, field.at[0:own], 0),
        move(pick_hbm, pick, 1),
        move(ztab_hbm.at[z_case], ztab, 2),
        move(xtab_hbm.at[x_case], xtab, 3),
        move(color_hbm, color, 4),
        move(ext_hbm, ext, 5),
        move(mat_hbm, mats, 6),
    ]
    for load in loads:
        load.start()

    loads[0].wait()
    loads[1].wait()
    picked = jnp.dot(
        pick[...], field[0:own, :], preferred_element_type=jnp.float32
    ).astype(jnp.bfloat16)
    edges[...] = picked[0 : 4 * zs]
    for n in range(4):
        corners[n] = picked[4 * zs + 8 * n : 4 * zs + 8 * n + 4]

    z_lo, z_hi = 0, 2 * xs
    x_lo = 4 * xs
    x_hi = x_lo + 2 * zs
    corner = x_hi + 2 * zs
    gathered = corner + 32
    def spread(ref, count, lo, hi):
        left, right = max(lo - LANES, 0), min(hi + LANES, cols)
        for r in range(0, count, 16):
            rows = ref[r : r + 16, left:right]
            first, final = rows[:, 0:LANES], rows[:, right - left - LANES :]
            nothing = jnp.zeros_like(first)
            at = lax.broadcasted_iota(jnp.int32, first.shape, 1)
            for k, shift in enumerate(SHIFTS):
                if shift == 0:
                    continue
                to = slice(k * count + r, k * count + r + 16)
                moved = pltpu.roll(rows, -shift % (right - left), 1)[:, lo - left : hi - left]
                ref[to, lo:hi] = moved
                if shift < 0 and lo == 0:
                    edge = jnp.where(at == -shift - 1, nothing, moved[:, 0:LANES])
                    if shift == -2:
                        edge = jnp.where(at == 0, -first, edge)
                    ref[to, 0:LANES] = edge
                if shift > 0 and hi == cols:
                    edge = jnp.where(at == LANES - shift, nothing, moved[:, hi - lo - LANES :])
                    if shift == 2:
                        edge = jnp.where(at == LANES - 1, -final, edge)
                    ref[to, cols - LANES : cols] = edge

    def local():
        loads[2].wait()
        loads[3].wait()
        for n, (_, _, y_taps) in enumerate(RESULTS):
            zc = ztab[n * zs : (n + 1) * zs, :]
            xc = xtab[n * xs : (n + 1) * xs, :]
            block = (zc[:, None, :] * xc[None, :, :]).reshape(own, own + gathered)
            rows = slice(n * own, (n + 1) * own)
            for k in range(len(SHIFTS)):
                scaled = (block * float(y_taps[SHIFTS[k] + 2])).astype(jnp.bfloat16)
                taps[rows, k * own : (k + 1) * own] = scaled[:, 0:own]
                halo_taps[rows, k * gathered : (k + 1) * gathered] = scaled[:, own:]

        wide = 2 * LANES
        spread(field, own, 0, cols)
        for t in range(cols // wide):
            at = slice(t * wide, (t + 1) * wide)
            filtered[:, at] = jnp.dot(taps[...], field[:, at], preferred_element_type=jnp.float32)

        total_z = zs * bricks
        for n in (4, 5, 6):
            loads[n].wait()
        levels = ext.shape[1]
        lut[...] = jnp.zeros_like(lut)
        lut[0:8, 0:levels] = jnp.broadcast_to(ext[...], (8, levels)) * (
            -2.0 / total_z * float(np.log2(np.e))
        )
        for c in range(3):
            lut[8 * c + 8 : 8 * c + 16, 0:levels] = jnp.broadcast_to(color[c : c + 1, :], (8, levels))

        def look(z, _):
            rows = pl.ds(pl.multiple_of(z * xs, 8), xs)
            for t in range(cols // LANES):
                tile = slice(t * LANES, (t + 1) * LANES)
                index = mats[rows, tile]
                for c in range(4):
                    looked[c, rows, tile] = jnp.take_along_axis(
                        lut[8 * c : 8 * c + 8, :], index, axis=1
                    )
            return 0

        lax.fori_loop(0, zs, look, 0)

    ahead = lax.rem(me_x, 24) < 2
    pl.when(ahead)(local)

    pl.semaphore_wait(barrier, len(sides))

    face = {
        (-1, 0): (dens_hbm.at[0 : 2 * xs], halo.at[z_hi : z_hi + 2 * xs]),
        (1, 0): (dens_hbm.at[own - 2 * xs : own], halo.at[z_lo : z_lo + 2 * xs]),
        (0, -1): (edges.at[0 : 2 * zs], halo.at[x_hi : x_hi + 2 * zs]),
        (0, 1): (edges.at[2 * zs : 4 * zs], halo.at[x_lo : x_lo + 2 * zs]),
        (-1, -1): (corners.at[0], corners_in.at[3]),
        (-1, 1): (corners.at[1], corners_in.at[2]),
        (1, -1): (corners.at[2], corners_in.at[1]),
        (1, 1): (corners.at[3], corners_in.at[0]),
    }
    halos = []
    for n, (dz, dx) in enumerate(sides):
        src, dst = face[dz, dx]
        halos.append(
            pltpu.make_async_remote_copy(
                src_ref=src,
                dst_ref=dst,
                send_sem=halo_send.at[n],
                recv_sem=halo_recv.at[n],
                device_id=device(dz, dx),
                device_id_type=MESH,
            )
        )
    for transfer in halos:
        transfer.start()

    rounds = bricks // 2 - 1

    def announce(r):
        for dz in (-1, 1):
            pl.semaphore_signal(ready.at[r], inc=1, device_id=device(dz, 0), device_id_type=MESH)

    announce(0)
    pl.when(jnp.logical_not(ahead))(local)
    for r in range(1, rounds):
        pl.semaphore_wait(ready.at[r - 1], 2)
        announce(r)

    for transfer in halos:
        transfer.wait()

    for n in range(4):
        halo[corner + 8 * n : corner + 8 * n + 8, :] = jnp.concatenate(
            [corners_in[n], jnp.zeros_like(corners_in[n])], axis=0
        )

    part = 2 * cols // bricks
    lane = lax.broadcasted_iota(jnp.int32, (xs, LANES), 1)
    low = lane < LANES // 2
    half = LANES // 2

    def encode(values):
        roots = jnp.sqrt(jnp.clip(jnp.concatenate(values, axis=0), 0.0, 1.0))
        return (jnp.round(roots * 65535.0) - 32768.0).astype(jnp.int32).astype(jnp.int16)

    def decode(code):
        roots = (code.astype(jnp.int32).astype(jnp.float32) + 32768.0) * (1.0 / 65535.0)
        return roots * roots

    def partial(dest):
        return pltpu.make_async_remote_copy(
            src_ref=send.at[dest],
            dst_ref=recv.at[me_z],
            send_sem=part_send.at[dest],
            recv_sem=part_recv.at[me_z],
            device_id=(dest, me_x),
            device_id_type=MESH,
        )

    pairs = bricks // 2
    mine = lax.div(me_z, 2)

    def pair_at(i):
        pair = 0
        for q in range(pairs):
            far = sorted(range(pairs), key=lambda p: (p != 0, -min((p - q) % pairs, (q - p) % pairs)))
            for k, p in enumerate(far):
                pair = jnp.where((mine == q) & (i == k), p, pair)
        return pair

    def render(pair):
        start = pl.multiple_of(pair * part, LANES) if not isinstance(pair, int) else pair * part
        at = pl.ds(start, part)
        chunk[...] = filtered[:, at] + jnp.dot(
            halo_taps[...], halo[:, at], preferred_element_type=jnp.float32
        )

        def cells(z, carry):
            clear, red, green, blue = carry
            row = pl.multiple_of(z * xs, 8)

            here = (pl.ds(row, xs), pl.ds(start, part))
            smooth, gz, gx, gy = [chunk[pl.ds(row + n * own, xs), :] for n in range(4)]
            lit = 0.35 + 0.65 * jnp.abs(LIGHT_Z * gz + LIGHT_X * gx + LIGHT_Y * gy) * lax.rsqrt(
                gz * gz + gx * gx + gy * gy + 1.0
            )
            passed = clear * jnp.exp2(looked[(0,) + here] * (smooth * smooth + 0.25))
            weight = (clear - passed) * lit
            return (
                passed,
                red + weight * looked[(1,) + here],
                green + weight * looked[(2,) + here],
                blue + weight * looked[(3,) + here],
            )

        def group(g, carry):
            for k in range(4):
                carry = cells(g * 4 + k, carry)
            return carry

        zero = jnp.zeros((xs, part), jnp.float32)
        clear, red, green, blue = lax.fori_loop(
            0, zs // 4, group, (zero + 1.0, zero, zero, zero)
        )
        result = (red, green, blue, 1.0 - clear)
        fronts = [v[:, 0:LANES] for v in result]
        mids = [v[:, LANES : 2 * LANES] for v in result]
        backs = [v[:, 2 * LANES : 3 * LANES] for v in result]
        swapped = [pltpu.roll(v, half, 1) for v in mids]
        even, odd = 2 * pair, 2 * pair + 1
        send[even] = encode(
            fronts + [jnp.where(low, mids[2 * c], swapped[2 * c + 1]) for c in (0, 1)]
        )
        send[odd] = encode(
            backs + [jnp.where(low, swapped[2 * c], mids[2 * c + 1]) for c in (0, 1)]
        )
        for dest in (even, odd):

            @pl.when(dest != me_z)
            def _():
                partial(dest).start()

        return 0

    spread(halo, gathered, 0, part)
    pl.semaphore_wait(ready.at[rounds - 1], 2)
    render(0)
    spread(halo, gathered, part, cols)
    lax.fori_loop(1, pairs, lambda i, _: render(pair_at(i)), 0)
    recv[me_z] = send[me_z]

    image = [jnp.zeros((xs, LANES), jnp.float32) for _ in range(5)]
    clear = jnp.ones((xs, LANES), jnp.float32)
    clear_half = clear
    for s in range(bricks):

        @pl.when(me_z != s)
        def _():
            pltpu.make_async_remote_copy(
                src_ref=send.at[s],
                dst_ref=recv.at[s],
                send_sem=part_send.at[s],
                recv_sem=part_recv.at[s],
                device_id=(s, me_x),
                device_id_type=MESH,
            ).wait()

        values = decode(recv[s])
        layer = [values[c * xs : (c + 1) * xs] for c in range(6)]
        for c in range(3):
            image[c] = image[c] + clear * layer[c]
        image[3] = image[3] + clear_half * layer[4]
        image[4] = image[4] + clear_half * layer[5]
        clear = clear * (1.0 - layer[3])
        clear_half = clear_half * (1.0 - jnp.where(low, pltpu.roll(layer[5], half, 1), layer[5]))
    mains = image[0:3] + [1.0 - clear]
    tail = jnp.where(low, image[4], 1.0 - clear_half)
    halves = [image[3], pltpu.roll(image[3], half, 1), tail, pltpu.roll(tail, half, 1)]
    is_even = lax.rem(me_z, 2) == 0
    for c in range(4):
        turned = pltpu.roll(mains[c], half, 1)
        out_ref[c, :, 0:LANES] = jnp.where(is_even, mains[c], jnp.where(low, halves[c], turned))
        out_ref[c, :, LANES : LANES + half] = jnp.where(is_even, halves[c], turned)[:, 0:half]


def shards(density, material, tf_color, tf_extinction):
    bricks = lax.axis_size("depth")
    planes = lax.axis_size("plane")
    zs, xs, cols = density.shape
    own = zs * xs
    ztab, xtab = tables(zs, xs)
    picker = edge_picker(zs, xs)
    gathered = ztab.shape[2] - own
    hbm = pl.BlockSpec(memory_space=pl.ANY)
    vmem = pl.BlockSpec(memory_space=pltpu.VMEM)
    shifts = len(SHIFTS)
    return pl.pallas_call(
        functools.partial(frame_kernel, zs, xs, cols, bricks, planes),
        out_shape=pltpu.VMEM((4, xs, cols // bricks), jnp.float32),
        in_specs=[hbm] * 7,
        out_specs=vmem,
        scratch_shapes=[
            pltpu.VMEM((shifts * own, cols), jnp.bfloat16),
            pltpu.VMEM((shifts * gathered, cols), jnp.bfloat16),
            pltpu.VMEM((own, cols), jnp.int32),
            pltpu.VMEM(tf_color.shape, jnp.float32),
            pltpu.VMEM((1, tf_extinction.shape[0]), jnp.float32),
            pltpu.VMEM(ztab.shape[1:], jnp.float32),
            pltpu.VMEM(xtab.shape[1:], jnp.float32),
            pltpu.VMEM(picker.shape, jnp.bfloat16),
            pltpu.VMEM((4 * zs, cols), jnp.bfloat16),
            pltpu.VMEM((4, 4, cols), jnp.bfloat16),
            pltpu.VMEM((4, 4, cols), jnp.bfloat16),
            pltpu.VMEM((4 * own, shifts * own), jnp.bfloat16),
            pltpu.VMEM((4 * own, shifts * gathered), jnp.bfloat16),
            pltpu.VMEM((4 * own, cols), jnp.float32),
            pltpu.VMEM((4 * own, 2 * cols // bricks), jnp.float32),
            pltpu.VMEM((4, own, cols), jnp.float32),
            pltpu.VMEM((32, LANES), jnp.float32),
            pltpu.VMEM((bricks, 6 * xs, LANES), jnp.int16),
            pltpu.VMEM((bricks, 6 * xs, LANES), jnp.int16),
            pltpu.SemaphoreType.DMA((7,)),
            pltpu.SemaphoreType.REGULAR((bricks // 2 - 1,)),
            pltpu.SemaphoreType.DMA((8,)),
            pltpu.SemaphoreType.DMA((8,)),
            pltpu.SemaphoreType.DMA((bricks,)),
            pltpu.SemaphoreType.DMA((bricks,)),
        ],
        compiler_params=pltpu.CompilerParams(collective_id=0, has_side_effects=True),
        name="frame",
    )(
        density.reshape(own, cols),
        material.reshape(own, cols),
        tf_color,
        tf_extinction.reshape(1, -1),
        jnp.asarray(ztab),
        jnp.asarray(xtab),
        jnp.asarray(picker, jnp.bfloat16),
    )


def solution(mesh):
    return jax.shard_map(
        shards,
        mesh=mesh,
        in_specs=(P("depth", "plane", None), P("depth", "plane", None), P(), P()),
        out_specs=P(None, "plane", "depth"),
        check_vma=False,
    )
```

```python
import functools

import jax
import jax.numpy as jnp
import numpy as np
from jax import lax
from jax.experimental import pallas as pl
from jax.experimental.pallas import tpu as pltpu
from jax.sharding import PartitionSpec as P

LIGHT_Z = 0.64
LIGHT_X = 0.48
LIGHT_Y = 0.6
LANES = 128
MESH = pl.DeviceIdType.MESH

TENT = np.array([0.0, 1.0, 2.0, 1.0, 0.0]) / 4.0
TENT_TENT = np.array([1.0, 4.0, 6.0, 4.0, 1.0]) / 16.0
SLOPE_TENT = np.array([-1.0, -2.0, 0.0, 2.0, 1.0]) / 8.0
RESULTS = (
    (TENT, TENT, TENT),
    (SLOPE_TENT, TENT_TENT, TENT_TENT),
    (TENT_TENT, SLOPE_TENT, TENT_TENT),
    (TENT_TENT, TENT_TENT, SLOPE_TENT),
)
SHIFTS = (0, -1, 1, -2, 2)


def banded(taps, count, case):
    matrix = np.zeros((count, count + 4))
    for o in range(count):
        matrix[o, o : o + 5] = taps
    if case == 0:
        matrix[:, 2] -= matrix[:, 0]
        matrix[:, 0:2] = 0.0
    if case == 2:
        matrix[:, count + 1] -= matrix[:, count + 3]
        matrix[:, count + 2 : count + 4] = 0.0
    return matrix


def gathered_rows(zs, xs):
    rows = [(z + 2, x + 2) for z in range(zs) for x in range(xs)]
    rows += [(z + 2, x) for z in range(zs) for x in (0, 1)]
    rows += [(z + 2, xs + 2 + x) for z in range(zs) for x in (0, 1)]
    rows += [(z, x + 2) for z in (0, 1) for x in range(xs)]
    rows += [(zs + 2 + z, x + 2) for z in (0, 1) for x in range(xs)]
    for z0 in (0, zs + 2):
        for x0 in (0, xs + 2):
            rows += [(z0 + z, x0 + x) for z in (0, 1) for x in (0, 1)]
            rows += [(-1, -1)] * 4
    return rows


def tables(zs, xs):
    rows = gathered_rows(zs, xs)
    zi = np.array([r[0] for r in rows])
    xi = np.array([r[1] for r in rows])
    keep = (zi >= 0).astype(np.float64)
    zi, xi = np.maximum(zi, 0), np.maximum(xi, 0)
    along_z = [
        np.concatenate([banded(taps[0], zs, case)[:, zi] for taps in RESULTS]) for case in range(3)
    ]
    along_x = [
        np.concatenate([banded(taps[1], xs, case)[:, xi] * keep for taps in RESULTS])
        for case in range(3)
    ]
    return np.stack(along_z).astype(np.float32), np.stack(along_x).astype(np.float32)


def edge_picker(zs, xs):
    own = {(z, x): z * xs + x for z in range(zs) for x in range(xs)}
    wanted = [own[z, x] for z in range(zs) for x in (0, 1)]
    wanted += [own[z, x] for z in range(zs) for x in (xs - 2, xs - 1)]
    for z0 in (0, zs - 2):
        for x0 in (0, xs - 2):
            wanted += [own[z0 + z, x0 + x] for z in (0, 1) for x in (0, 1)]
            wanted += [-1] * 4
    picker = np.zeros((len(wanted), zs * xs), np.float32)
    for row, source in enumerate(wanted):
        if source >= 0:
            picker[row, source] = 1.0
    return picker


def frame_kernel(
    zs, xs, cols, bricks, planes,
    dens_hbm, mat_hbm, color_hbm, ext_hbm, ztab_hbm, xtab_hbm, pick_hbm,
    out_ref,
    field, halo_x, halo_z, mats, color, ext, ztab, xtab, pick, edges, corners, corners_in, taps, taps_x, taps_z,
    filtered, chunk, looked, lut, send, recv,
    load_sem, ready, halo_send, halo_recv, part_send, part_recv,
):
    own = zs * xs
    me_z = lax.axis_index("depth")
    me_x = lax.axis_index("plane")

    def device(dz, dx):
        return (lax.rem(me_z + dz + bricks, bricks), lax.rem(me_x + dx + planes, planes))

    sides = [(0, -1), (0, 1), (-1, -1), (-1, 1), (1, -1), (1, 1), (-1, 0), (1, 0)]
    barrier = pltpu.get_barrier_semaphore()
    for dz, dx in sides:
        pl.semaphore_signal(barrier, inc=1, device_id=device(dz, dx), device_id_type=MESH)

    def move(src, dst, sem):
        return pltpu.make_async_copy(src, dst, load_sem.at[sem])

    z_case = jnp.where(me_z == 0, 0, jnp.where(me_z == bricks - 1, 2, 1))
    x_case = jnp.where(me_x == 0, 0, jnp.where(me_x == planes - 1, 2, 1))
    loads = [
        move(dens_hbm, field.at[0:own], 0),
        move(pick_hbm, pick, 1),
        move(ztab_hbm.at[z_case], ztab, 2),
        move(xtab_hbm.at[x_case], xtab, 3),
        move(color_hbm, color, 4),
        move(ext_hbm, ext, 5),
        move(mat_hbm, mats, 6),
    ]
    for load in loads:
        load.start()

    loads[0].wait()
    loads[1].wait()
    picked = jnp.dot(
        pick[...], field[0:own, :], preferred_element_type=jnp.float32
    ).astype(jnp.bfloat16)
    edges[...] = picked[0 : 4 * zs]
    for n in range(4):
        corners[n] = picked[4 * zs + 8 * n : 4 * zs + 8 * n + 4]

    x_lo, x_hi = 0, 2 * zs
    z_lo, z_hi, corner = 0, 2 * xs, 4 * xs
    beside = 4 * zs
    gathered = corner + 32

    def spread(ref, count, lo, hi):
        left, right = max(lo - LANES, 0), min(hi + LANES, cols)
        for r in range(0, count, 16):
            rows = ref[r : r + 16, left:right]
            first, final = rows[:, 0:LANES], rows[:, right - left - LANES :]
            nothing = jnp.zeros_like(first)
            at = lax.broadcasted_iota(jnp.int32, first.shape, 1)
            for k, shift in enumerate(SHIFTS):
                if shift == 0:
                    continue
                to = slice(k * count + r, k * count + r + 16)
                moved = pltpu.roll(rows, -shift % (right - left), 1)[:, lo - left : hi - left]
                ref[to, lo:hi] = moved
                if shift < 0 and lo == 0:
                    edge = jnp.where(at == -shift - 1, nothing, moved[:, 0:LANES])
                    if shift == -2:
                        edge = jnp.where(at == 0, -first, edge)
                    ref[to, 0:LANES] = edge
                if shift > 0 and hi == cols:
                    edge = jnp.where(at == LANES - shift, nothing, moved[:, hi - lo - LANES :])
                    if shift == 2:
                        edge = jnp.where(at == LANES - 1, -final, edge)
                    ref[to, cols - LANES : cols] = edge

    def local():
        loads[2].wait()
        loads[3].wait()
        for n, (_, _, y_taps) in enumerate(RESULTS):
            zc = ztab[n * zs : (n + 1) * zs, :]
            xc = xtab[n * xs : (n + 1) * xs, :]
            block = (zc[:, None, :] * xc[None, :, :]).reshape(own, own + beside + gathered)
            rows = slice(n * own, (n + 1) * own)
            for k in range(len(SHIFTS)):
                scaled = (block * float(y_taps[SHIFTS[k] + 2])).astype(jnp.bfloat16)
                taps[rows, k * own : (k + 1) * own] = scaled[:, 0:own]
                taps_x[rows, k * beside : (k + 1) * beside] = scaled[:, own : own + beside]
                ends = slice(k * gathered, (k + 1) * gathered)
                taps_z[n * 4 * xs : n * 4 * xs + 2 * xs, ends] = scaled[0 : 2 * xs, own + beside :]
                taps_z[n * 4 * xs + 2 * xs : (n + 1) * 4 * xs, ends] = scaled[own - 2 * xs :, own + beside :]

        wide = 2 * LANES
        spread(field, own, 0, cols)
        for t in range(cols // wide):
            at = slice(t * wide, (t + 1) * wide)
            filtered[:, at] = jnp.dot(taps[...], field[:, at], preferred_element_type=jnp.float32)

        total_z = zs * bricks
        for n in (4, 5, 6):
            loads[n].wait()
        levels = ext.shape[1]
        lut[...] = jnp.zeros_like(lut)
        lut[0:8, 0:levels] = jnp.broadcast_to(ext[...], (8, levels)) * (
            -2.0 / total_z * float(np.log2(np.e))
        )
        for c in range(3):
            lut[8 * c + 8 : 8 * c + 16, 0:levels] = jnp.broadcast_to(color[c : c + 1, :], (8, levels))

        def look(z, _):
            rows = pl.ds(pl.multiple_of(z * xs, 8), xs)
            for t in range(cols // LANES):
                tile = slice(t * LANES, (t + 1) * LANES)
                index = mats[rows, tile]
                for c in range(4):
                    looked[c, rows, tile] = jnp.take_along_axis(
                        lut[8 * c : 8 * c + 8, :], index, axis=1
                    )
            return 0

        lax.fori_loop(0, zs, look, 0)

    ahead = lax.rem(me_x, 24) < 2
    pl.when(ahead)(local)

    pl.semaphore_wait(barrier, len(sides))

    face = {
        (-1, 0): (dens_hbm.at[0 : 2 * xs], halo_z.at[z_hi : z_hi + 2 * xs]),
        (1, 0): (dens_hbm.at[own - 2 * xs : own], halo_z.at[z_lo : z_lo + 2 * xs]),
        (0, -1): (edges.at[0 : 2 * zs], halo_x.at[x_hi : x_hi + 2 * zs]),
        (0, 1): (edges.at[2 * zs : 4 * zs], halo_x.at[x_lo : x_lo + 2 * zs]),
        (-1, -1): (corners.at[0], corners_in.at[3]),
        (-1, 1): (corners.at[1], corners_in.at[2]),
        (1, -1): (corners.at[2], corners_in.at[1]),
        (1, 1): (corners.at[3], corners_in.at[0]),
    }
    halos = []
    for n, (dz, dx) in enumerate(sides):
        src, dst = face[dz, dx]
        halos.append(
            pltpu.make_async_remote_copy(
                src_ref=src,
                dst_ref=dst,
                send_sem=halo_send.at[n],
                recv_sem=halo_recv.at[n],
                device_id=device(dz, dx),
                device_id_type=MESH,
            )
        )
    for transfer in halos:
        transfer.start()

    rounds = bricks // 2 - 1

    def announce(r):
        for dz in (-1, 1):
            pl.semaphore_signal(ready.at[r], inc=1, device_id=device(dz, 0), device_id_type=MESH)

    announce(0)
    pl.when(jnp.logical_not(ahead))(local)
    for r in range(1, rounds):
        pl.semaphore_wait(ready.at[r - 1], 2)
        announce(r)

    for transfer in halos[0:2]:
        transfer.wait_recv()
    spread(halo_x, beside, 0, cols)
    for transfer in halos[2:]:
        transfer.wait_recv()

    for n in range(4):
        halo_z[corner + 8 * n : corner + 8 * n + 8, :] = jnp.concatenate(
            [corners_in[n], jnp.zeros_like(corners_in[n])], axis=0
        )

    part = 2 * cols // bricks
    lane = lax.broadcasted_iota(jnp.int32, (xs, LANES), 1)
    low = lane < LANES // 2
    half = LANES // 2

    def encode(values):
        roots = jnp.sqrt(jnp.clip(jnp.concatenate(values, axis=0), 0.0, 1.0))
        return (jnp.round(roots * 65535.0) - 32768.0).astype(jnp.int32).astype(jnp.int16)

    def decode(code):
        roots = (code.astype(jnp.int32).astype(jnp.float32) + 32768.0) * (1.0 / 65535.0)
        return roots * roots

    def partial(dest):
        return pltpu.make_async_remote_copy(
            src_ref=send.at[dest],
            dst_ref=recv.at[me_z],
            send_sem=part_send.at[dest],
            recv_sem=part_recv.at[me_z],
            device_id=(dest, me_x),
            device_id_type=MESH,
        )

    pairs = bricks // 2
    mine = lax.div(me_z, 2)

    def pair_at(i):
        pair = 0
        for q in range(pairs):
            far = sorted(range(pairs), key=lambda p: (p != 0, -min((p - q) % pairs, (q - p) % pairs)))
            for k, p in enumerate(far):
                pair = jnp.where((mine == q) & (i == k), p, pair)
        return pair

    def render(pair):
        start = pl.multiple_of(pair * part, LANES) if not isinstance(pair, int) else pair * part
        at = pl.ds(start, part)
        chunk[...] = filtered[:, at] + jnp.dot(
            taps_x[...], halo_x[:, at], preferred_element_type=jnp.float32
        )
        ends = jnp.dot(taps_z[...], halo_z[:, at], preferred_element_type=jnp.float32)
        for n in range(4):
            for k, row in enumerate((n * own, (n + 1) * own - 2 * xs)):
                from_row = (2 * n + k) * 2 * xs
                rows = slice(row, row + 2 * xs)
                chunk[rows, :] = chunk[rows, :] + ends[from_row : from_row + 2 * xs]

        def cells(z, carry):
            clear, red, green, blue = carry
            row = pl.multiple_of(z * xs, 8)

            here = (pl.ds(row, xs), pl.ds(start, part))
            smooth, gz, gx, gy = [chunk[pl.ds(row + n * own, xs), :] for n in range(4)]
            lit = 0.35 + 0.65 * jnp.abs(LIGHT_Z * gz + LIGHT_X * gx + LIGHT_Y * gy) * lax.rsqrt(
                gz * gz + gx * gx + gy * gy + 1.0
            )
            passed = clear * jnp.exp2(looked[(0,) + here] * (smooth * smooth + 0.25))
            weight = (clear - passed) * lit
            return (
                passed,
                red + weight * looked[(1,) + here],
                green + weight * looked[(2,) + here],
                blue + weight * looked[(3,) + here],
            )

        def group(g, carry):
            for k in range(4):
                carry = cells(g * 4 + k, carry)
            return carry

        zero = jnp.zeros((xs, part), jnp.float32)
        clear, red, green, blue = lax.fori_loop(
            0, zs // 4, group, (zero + 1.0, zero, zero, zero)
        )
        result = (red, green, blue, 1.0 - clear)
        fronts = [v[:, 0:LANES] for v in result]
        mids = [v[:, LANES : 2 * LANES] for v in result]
        backs = [v[:, 2 * LANES : 3 * LANES] for v in result]
        swapped = [pltpu.roll(v, half, 1) for v in mids]
        even, odd = 2 * pair, 2 * pair + 1
        send[even] = encode(
            fronts + [jnp.where(low, mids[2 * c], swapped[2 * c + 1]) for c in (0, 1)]
        )
        send[odd] = encode(
            backs + [jnp.where(low, swapped[2 * c], mids[2 * c + 1]) for c in (0, 1)]
        )
        for dest in (even, odd):

            @pl.when(dest != me_z)
            def _():
                partial(dest).start()

        return 0

    spread(halo_z, gathered, 0, part)
    pl.semaphore_wait(ready.at[rounds - 1], 2)
    render(0)
    spread(halo_z, gathered, part, cols)
    lax.fori_loop(1, pairs, lambda i, _: render(pair_at(i)), 0)
    recv[me_z] = send[me_z]
    for transfer in halos:
        transfer.wait_send()

    image = [jnp.zeros((xs, LANES), jnp.float32) for _ in range(5)]
    clear = jnp.ones((xs, LANES), jnp.float32)
    clear_half = clear
    for s in range(bricks):

        @pl.when(me_z != s)
        def _():
            pltpu.make_async_remote_copy(
                src_ref=send.at[s],
                dst_ref=recv.at[s],
                send_sem=part_send.at[s],
                recv_sem=part_recv.at[s],
                device_id=(s, me_x),
                device_id_type=MESH,
            ).wait()

        values = decode(recv[s])
        layer = [values[c * xs : (c + 1) * xs] for c in range(6)]
        for c in range(3):
            image[c] = image[c] + clear * layer[c]
        image[3] = image[3] + clear_half * layer[4]
        image[4] = image[4] + clear_half * layer[5]
        clear = clear * (1.0 - layer[3])
        clear_half = clear_half * (1.0 - jnp.where(low, pltpu.roll(layer[5], half, 1), layer[5]))
    mains = image[0:3] + [1.0 - clear]
    tail = jnp.where(low, image[4], 1.0 - clear_half)
    halves = [image[3], pltpu.roll(image[3], half, 1), tail, pltpu.roll(tail, half, 1)]
    is_even = lax.rem(me_z, 2) == 0
    for c in range(4):
        turned = pltpu.roll(mains[c], half, 1)
        out_ref[c, :, 0:LANES] = jnp.where(is_even, mains[c], jnp.where(low, halves[c], turned))
        out_ref[c, :, LANES : LANES + half] = jnp.where(is_even, halves[c], turned)[:, 0:half]


def shards(density, material, tf_color, tf_extinction):
    bricks = lax.axis_size("depth")
    planes = lax.axis_size("plane")
    zs, xs, cols = density.shape
    own = zs * xs
    ztab, xtab = tables(zs, xs)
    picker = edge_picker(zs, xs)
    gathered = ztab.shape[2] - own - 4 * zs
    hbm = pl.BlockSpec(memory_space=pl.ANY)
    vmem = pl.BlockSpec(memory_space=pltpu.VMEM)
    shifts = len(SHIFTS)
    return pl.pallas_call(
        functools.partial(frame_kernel, zs, xs, cols, bricks, planes),
        out_shape=pltpu.VMEM((4, xs, cols // bricks), jnp.float32),
        in_specs=[hbm] * 7,
        out_specs=vmem,
        scratch_shapes=[
            pltpu.VMEM((shifts * own, cols), jnp.bfloat16),
            pltpu.VMEM((shifts * 4 * zs, cols), jnp.bfloat16),
            pltpu.VMEM((shifts * gathered, cols), jnp.bfloat16),
            pltpu.VMEM((own, cols), jnp.int32),
            pltpu.VMEM(tf_color.shape, jnp.float32),
            pltpu.VMEM((1, tf_extinction.shape[0]), jnp.float32),
            pltpu.VMEM(ztab.shape[1:], jnp.float32),
            pltpu.VMEM(xtab.shape[1:], jnp.float32),
            pltpu.VMEM(picker.shape, jnp.bfloat16),
            pltpu.VMEM((4 * zs, cols), jnp.bfloat16),
            pltpu.VMEM((4, 4, cols), jnp.bfloat16),
            pltpu.VMEM((4, 4, cols), jnp.bfloat16),
            pltpu.VMEM((4 * own, shifts * own), jnp.bfloat16),
            pltpu.VMEM((4 * own, shifts * 4 * zs), jnp.bfloat16),
            pltpu.VMEM((16 * xs, shifts * gathered), jnp.bfloat16),
            pltpu.VMEM((4 * own, cols), jnp.float32),
            pltpu.VMEM((4 * own, 2 * cols // bricks), jnp.float32),
            pltpu.VMEM((4, own, cols), jnp.float32),
            pltpu.VMEM((32, LANES), jnp.float32),
            pltpu.VMEM((bricks, 6 * xs, LANES), jnp.int16),
            pltpu.VMEM((bricks, 6 * xs, LANES), jnp.int16),
            pltpu.SemaphoreType.DMA((7,)),
            pltpu.SemaphoreType.REGULAR((bricks // 2 - 1,)),
            pltpu.SemaphoreType.DMA((8,)),
            pltpu.SemaphoreType.DMA((8,)),
            pltpu.SemaphoreType.DMA((bricks,)),
            pltpu.SemaphoreType.DMA((bricks,)),
        ],
        compiler_params=pltpu.CompilerParams(collective_id=0, has_side_effects=True),
        name="frame",
    )(
        density.reshape(own, cols),
        material.reshape(own, cols),
        tf_color,
        tf_extinction.reshape(1, -1),
        jnp.asarray(ztab),
        jnp.asarray(xtab),
        jnp.asarray(picker, jnp.bfloat16),
    )


def solution(mesh):
    return jax.shard_map(
        shards,
        mesh=mesh,
        in_specs=(P("depth", "plane", None), P("depth", "plane", None), P(), P()),
        out_specs=P(None, "plane", "depth"),
        check_vma=False,
    )
```

```python
import functools

import jax
import jax.numpy as jnp
import numpy as np
from jax import lax
from jax.experimental import pallas as pl
from jax.experimental.pallas import tpu as pltpu
from jax.sharding import PartitionSpec as P

LIGHT_Z = 0.64
LIGHT_X = 0.48
LIGHT_Y = 0.6
LANES = 128
MESH = pl.DeviceIdType.MESH

TENT = np.array([0.0, 1.0, 2.0, 1.0, 0.0]) / 4.0
TENT_TENT = np.array([1.0, 4.0, 6.0, 4.0, 1.0]) / 16.0
SLOPE_TENT = np.array([-1.0, -2.0, 0.0, 2.0, 1.0]) / 8.0
RESULTS = (
    (TENT, TENT, TENT),
    (SLOPE_TENT, TENT_TENT, TENT_TENT),
    (TENT_TENT, SLOPE_TENT, TENT_TENT),
    (TENT_TENT, TENT_TENT, SLOPE_TENT),
)
SHIFTS = (0, -1, 1, -2, 2)


def banded(taps, count, case):
    matrix = np.zeros((count, count + 4))
    for o in range(count):
        matrix[o, o : o + 5] = taps
    if case == 0:
        matrix[:, 2] -= matrix[:, 0]
        matrix[:, 0:2] = 0.0
    if case == 2:
        matrix[:, count + 1] -= matrix[:, count + 3]
        matrix[:, count + 2 : count + 4] = 0.0
    return matrix


def gathered_rows(zs, xs):
    rows = [(z + 2, x + 2) for z in range(zs) for x in range(xs)]
    rows += [(z + 2, x) for z in range(zs) for x in (0, 1)]
    rows += [(z + 2, xs + 2 + x) for z in range(zs) for x in (0, 1)]
    rows += [(z, x + 2) for z in (0, 1) for x in range(xs)]
    rows += [(zs + 2 + z, x + 2) for z in (0, 1) for x in range(xs)]
    for z0 in (0, zs + 2):
        for x0 in (0, xs + 2):
            rows += [(z0 + z, x0 + x) for z in (0, 1) for x in (0, 1)]
            rows += [(-1, -1)] * 4
    return rows


def tables(zs, xs):
    rows = gathered_rows(zs, xs)
    zi = np.array([r[0] for r in rows])
    xi = np.array([r[1] for r in rows])
    keep = (zi >= 0).astype(np.float64)
    zi, xi = np.maximum(zi, 0), np.maximum(xi, 0)
    along_z = [
        np.concatenate([banded(taps[0], zs, case)[:, zi] for taps in RESULTS]) for case in range(3)
    ]
    along_x = [
        np.concatenate([banded(taps[1], xs, case)[:, xi] * keep for taps in RESULTS])
        for case in range(3)
    ]
    return np.stack(along_z).astype(np.float32), np.stack(along_x).astype(np.float32)


def edge_picker(zs, xs):
    own = {(z, x): z * xs + x for z in range(zs) for x in range(xs)}
    wanted = [own[z, x] for z in range(zs) for x in (0, 1)]
    wanted += [own[z, x] for z in range(zs) for x in (xs - 2, xs - 1)]
    for z0 in (0, zs - 2):
        for x0 in (0, xs - 2):
            wanted += [own[z0 + z, x0 + x] for z in (0, 1) for x in (0, 1)]
            wanted += [-1] * 4
    picker = np.zeros((len(wanted), zs * xs), np.float32)
    for row, source in enumerate(wanted):
        if source >= 0:
            picker[row, source] = 1.0
    return picker


def frame_kernel(
    zs, xs, cols, bricks, planes,
    dens_hbm, mat_hbm, color_hbm, ext_hbm, ztab_hbm, xtab_hbm, pick_hbm,
    out_ref,
    field, halo_x, halo_z, mats, color, ext, ztab, xtab, pick, edges, corners, corners_in, taps, taps_x, taps_z,
    filtered, chunk, looked, lut, send, recv,
    load_sem, ready, halo_send, halo_recv, part_send, part_recv,
):
    own = zs * xs
    me_z = lax.axis_index("depth")
    me_x = lax.axis_index("plane")

    def device(dz, dx):
        return (lax.rem(me_z + dz + bricks, bricks), lax.rem(me_x + dx + planes, planes))

    sides = [(0, -1), (0, 1), (-1, -1), (-1, 1), (1, -1), (1, 1), (-1, 0), (1, 0)]
    def move(src, dst, sem):
        return pltpu.make_async_copy(src, dst, load_sem.at[sem])

    z_case = jnp.where(me_z == 0, 0, jnp.where(me_z == bricks - 1, 2, 1))
    x_case = jnp.where(me_x == 0, 0, jnp.where(me_x == planes - 1, 2, 1))
    loads = [
        move(dens_hbm, field.at[0:own], 0),
        move(pick_hbm, pick, 1),
        move(ztab_hbm.at[z_case], ztab, 2),
        move(xtab_hbm.at[x_case], xtab, 3),
        move(color_hbm, color, 4),
        move(ext_hbm, ext, 5),
        move(mat_hbm, mats, 6),
    ]
    for load in loads[0:2]:
        load.start()

    barrier = pltpu.get_barrier_semaphore()
    for dz, dx in sides:
        pl.semaphore_signal(barrier, inc=1, device_id=device(dz, dx), device_id_type=MESH)

    for load in loads[2:]:
        load.start()

    loads[0].wait()
    loads[1].wait()
    picked = jnp.dot(
        pick[...], field[0:own, :], preferred_element_type=jnp.float32
    ).astype(jnp.bfloat16)
    edges[...] = picked[0 : 4 * zs]
    for n in range(4):
        corners[n] = picked[4 * zs + 8 * n : 4 * zs + 8 * n + 4]

    x_lo, x_hi = 0, 2 * zs
    z_lo, z_hi, corner = 0, 2 * xs, 4 * xs
    beside = 4 * zs
    gathered = corner + 32

    def spread(ref, count, lo, hi):
        left, right = max(lo - LANES, 0), min(hi + LANES, cols)
        for r in range(0, count, 16):
            rows = ref[r : r + 16, left:right]
            first, final = rows[:, 0:LANES], rows[:, right - left - LANES :]
            nothing = jnp.zeros_like(first)
            at = lax.broadcasted_iota(jnp.int32, first.shape, 1)
            for k, shift in enumerate(SHIFTS):
                if shift == 0:
                    continue
                to = slice(k * count + r, k * count + r + 16)
                moved = pltpu.roll(rows, -shift % (right - left), 1)[:, lo - left : hi - left]
                ref[to, lo:hi] = moved
                if shift < 0 and lo == 0:
                    edge = jnp.where(at == -shift - 1, nothing, moved[:, 0:LANES])
                    if shift == -2:
                        edge = jnp.where(at == 0, -first, edge)
                    ref[to, 0:LANES] = edge
                if shift > 0 and hi == cols:
                    edge = jnp.where(at == LANES - shift, nothing, moved[:, hi - lo - LANES :])
                    if shift == 2:
                        edge = jnp.where(at == LANES - 1, -final, edge)
                    ref[to, cols - LANES : cols] = edge

    def local():
        loads[2].wait()
        loads[3].wait()
        for n, (_, _, y_taps) in enumerate(RESULTS):
            zc = ztab[n * zs : (n + 1) * zs, :]
            xc = xtab[n * xs : (n + 1) * xs, :]
            block = (zc[:, None, :] * xc[None, :, :]).reshape(own, own + beside + gathered)
            rows = slice(n * own, (n + 1) * own)
            for k in range(len(SHIFTS)):
                scaled = (block * float(y_taps[SHIFTS[k] + 2])).astype(jnp.bfloat16)
                taps[rows, k * own : (k + 1) * own] = scaled[:, 0:own]
                taps_x[rows, k * beside : (k + 1) * beside] = scaled[:, own : own + beside]
                ends = slice(k * gathered, (k + 1) * gathered)
                taps_z[n * 4 * xs : n * 4 * xs + 2 * xs, ends] = scaled[0 : 2 * xs, own + beside :]
                taps_z[n * 4 * xs + 2 * xs : (n + 1) * 4 * xs, ends] = scaled[own - 2 * xs :, own + beside :]

        wide = 2 * LANES
        spread(field, own, 0, cols)
        for t in range(cols // wide):
            at = slice(t * wide, (t + 1) * wide)
            filtered[:, at] = jnp.dot(taps[...], field[:, at], preferred_element_type=jnp.float32)

        total_z = zs * bricks
        for n in (4, 5, 6):
            loads[n].wait()
        levels = ext.shape[1]
        lut[...] = jnp.zeros_like(lut)
        lut[0:8, 0:levels] = jnp.broadcast_to(ext[...], (8, levels)) * (
            -2.0 / total_z * float(np.log2(np.e))
        )
        for c in range(3):
            lut[8 * c + 8 : 8 * c + 16, 0:levels] = jnp.broadcast_to(color[c : c + 1, :], (8, levels))

        def look(z, _):
            rows = pl.ds(pl.multiple_of(z * xs, 8), xs)
            for t in range(cols // LANES):
                tile = slice(t * LANES, (t + 1) * LANES)
                index = mats[rows, tile]
                for c in range(4):
                    looked[c, rows, tile] = jnp.take_along_axis(
                        lut[8 * c : 8 * c + 8, :], index, axis=1
                    )
            return 0

        lax.fori_loop(0, zs, look, 0)

    ahead = lax.rem(me_x, 24) < 2
    pl.when(ahead)(local)

    pl.semaphore_wait(barrier, len(sides))

    face = {
        (-1, 0): (dens_hbm.at[0 : 2 * xs], halo_z.at[z_hi : z_hi + 2 * xs]),
        (1, 0): (dens_hbm.at[own - 2 * xs : own], halo_z.at[z_lo : z_lo + 2 * xs]),
        (0, -1): (edges.at[0 : 2 * zs], halo_x.at[x_hi : x_hi + 2 * zs]),
        (0, 1): (edges.at[2 * zs : 4 * zs], halo_x.at[x_lo : x_lo + 2 * zs]),
        (-1, -1): (corners.at[0], corners_in.at[3]),
        (-1, 1): (corners.at[1], corners_in.at[2]),
        (1, -1): (corners.at[2], corners_in.at[1]),
        (1, 1): (corners.at[3], corners_in.at[0]),
    }
    halos = []
    for n, (dz, dx) in enumerate(sides):
        src, dst = face[dz, dx]
        halos.append(
            pltpu.make_async_remote_copy(
                src_ref=src,
                dst_ref=dst,
                send_sem=halo_send.at[n],
                recv_sem=halo_recv.at[n],
                device_id=device(dz, dx),
                device_id_type=MESH,
            )
        )
    for transfer in halos:
        transfer.start()

    rounds = bricks // 2 - 1

    def announce(r):
        for dz in (-1, 1):
            pl.semaphore_signal(ready.at[r], inc=1, device_id=device(dz, 0), device_id_type=MESH)

    announce(0)
    pl.when(jnp.logical_not(ahead))(local)
    for r in range(1, rounds):
        pl.semaphore_wait(ready.at[r - 1], 2)
        announce(r)

    for transfer in halos[0:2]:
        transfer.wait_recv()
    spread(halo_x, beside, 0, cols)
    for transfer in halos[2:]:
        transfer.wait_recv()

    for n in range(4):
        halo_z[corner + 8 * n : corner + 8 * n + 8, :] = jnp.concatenate(
            [corners_in[n], jnp.zeros_like(corners_in[n])], axis=0
        )

    part = 2 * cols // bricks
    lane = lax.broadcasted_iota(jnp.int32, (xs, LANES), 1)
    low = lane < LANES // 2
    half = LANES // 2

    def encode(values):
        roots = jnp.sqrt(jnp.clip(jnp.concatenate(values, axis=0), 0.0, 1.0))
        return (jnp.round(roots * 65535.0) - 32768.0).astype(jnp.int32).astype(jnp.int16)

    def decode(code):
        roots = (code.astype(jnp.int32).astype(jnp.float32) + 32768.0) * (1.0 / 65535.0)
        return roots * roots

    def partial(dest):
        return pltpu.make_async_remote_copy(
            src_ref=send.at[dest],
            dst_ref=recv.at[me_z],
            send_sem=part_send.at[dest],
            recv_sem=part_recv.at[me_z],
            device_id=(dest, me_x),
            device_id_type=MESH,
        )

    pairs = bricks // 2
    mine = lax.div(me_z, 2)

    def pair_at(i):
        pair = 0
        for q in range(pairs):
            far = sorted(range(pairs), key=lambda p: (p != 0, -min((p - q) % pairs, (q - p) % pairs)))
            for k, p in enumerate(far):
                pair = jnp.where((mine == q) & (i == k), p, pair)
        return pair

    def render(pair):
        start = pl.multiple_of(pair * part, LANES) if not isinstance(pair, int) else pair * part
        at = pl.ds(start, part)
        chunk[...] = filtered[:, at] + jnp.dot(
            taps_x[...], halo_x[:, at], preferred_element_type=jnp.float32
        )
        ends = jnp.dot(taps_z[...], halo_z[:, at], preferred_element_type=jnp.float32)
        for n in range(4):
            for k, row in enumerate((n * own, (n + 1) * own - 2 * xs)):
                from_row = (2 * n + k) * 2 * xs
                rows = slice(row, row + 2 * xs)
                chunk[rows, :] = chunk[rows, :] + ends[from_row : from_row + 2 * xs]

        def cells(z, carry):
            clear, red, green, blue = carry
            row = pl.multiple_of(z * xs, 8)

            here = (pl.ds(row, xs), pl.ds(start, part))
            smooth, gz, gx, gy = [chunk[pl.ds(row + n * own, xs), :] for n in range(4)]
            lit = 0.35 + 0.65 * jnp.abs(LIGHT_Z * gz + LIGHT_X * gx + LIGHT_Y * gy) * lax.rsqrt(
                gz * gz + gx * gx + gy * gy + 1.0
            )
            passed = clear * jnp.exp2(looked[(0,) + here] * (smooth * smooth + 0.25))
            weight = (clear - passed) * lit
            return (
                passed,
                red + weight * looked[(1,) + here],
                green + weight * looked[(2,) + here],
                blue + weight * looked[(3,) + here],
            )

        def group(g, carry):
            for k in range(4):
                carry = cells(g * 4 + k, carry)
            return carry

        zero = jnp.zeros((xs, part), jnp.float32)
        clear, red, green, blue = lax.fori_loop(
            0, zs // 4, group, (zero + 1.0, zero, zero, zero)
        )
        result = (red, green, blue, 1.0 - clear)
        fronts = [v[:, 0:LANES] for v in result]
        mids = [v[:, LANES : 2 * LANES] for v in result]
        backs = [v[:, 2 * LANES : 3 * LANES] for v in result]
        swapped = [pltpu.roll(v, half, 1) for v in mids]
        even, odd = 2 * pair, 2 * pair + 1
        send[even] = encode(
            fronts + [jnp.where(low, mids[2 * c], swapped[2 * c + 1]) for c in (0, 1)]
        )
        send[odd] = encode(
            backs + [jnp.where(low, swapped[2 * c], mids[2 * c + 1]) for c in (0, 1)]
        )
        for dest in (even, odd):

            @pl.when(dest != me_z)
            def _():
                partial(dest).start()

        return 0

    spread(halo_z, gathered, 0, part)
    pl.semaphore_wait(ready.at[rounds - 1], 2)
    render(0)
    spread(halo_z, gathered, part, cols)
    lax.fori_loop(1, pairs, lambda i, _: render(pair_at(i)), 0)
    recv[me_z] = send[me_z]
    for transfer in halos:
        transfer.wait_send()

    image = [jnp.zeros((xs, LANES), jnp.float32) for _ in range(5)]
    clear = jnp.ones((xs, LANES), jnp.float32)
    clear_half = clear
    for s in range(bricks):

        @pl.when(me_z != s)
        def _():
            pltpu.make_async_remote_copy(
                src_ref=send.at[s],
                dst_ref=recv.at[s],
                send_sem=part_send.at[s],
                recv_sem=part_recv.at[s],
                device_id=(s, me_x),
                device_id_type=MESH,
            ).wait()

        values = decode(recv[s])
        layer = [values[c * xs : (c + 1) * xs] for c in range(6)]
        for c in range(3):
            image[c] = image[c] + clear * layer[c]
        image[3] = image[3] + clear_half * layer[4]
        image[4] = image[4] + clear_half * layer[5]
        clear = clear * (1.0 - layer[3])
        clear_half = clear_half * (1.0 - jnp.where(low, pltpu.roll(layer[5], half, 1), layer[5]))
    mains = image[0:3] + [1.0 - clear]
    tail = jnp.where(low, image[4], 1.0 - clear_half)
    halves = [image[3], pltpu.roll(image[3], half, 1), tail, pltpu.roll(tail, half, 1)]
    is_even = lax.rem(me_z, 2) == 0
    for c in range(4):
        turned = pltpu.roll(mains[c], half, 1)
        out_ref[c, :, 0:LANES] = jnp.where(is_even, mains[c], jnp.where(low, halves[c], turned))
        out_ref[c, :, LANES : LANES + half] = jnp.where(is_even, halves[c], turned)[:, 0:half]


def shards(density, material, tf_color, tf_extinction):
    bricks = lax.axis_size("depth")
    planes = lax.axis_size("plane")
    zs, xs, cols = density.shape
    own = zs * xs
    ztab, xtab = tables(zs, xs)
    picker = edge_picker(zs, xs)
    gathered = ztab.shape[2] - own - 4 * zs
    hbm = pl.BlockSpec(memory_space=pl.ANY)
    vmem = pl.BlockSpec(memory_space=pltpu.VMEM)
    shifts = len(SHIFTS)
    return pl.pallas_call(
        functools.partial(frame_kernel, zs, xs, cols, bricks, planes),
        out_shape=pltpu.VMEM((4, xs, cols // bricks), jnp.float32),
        in_specs=[hbm] * 7,
        out_specs=vmem,
        scratch_shapes=[
            pltpu.VMEM((shifts * own, cols), jnp.bfloat16),
            pltpu.VMEM((shifts * 4 * zs, cols), jnp.bfloat16),
            pltpu.VMEM((shifts * gathered, cols), jnp.bfloat16),
            pltpu.VMEM((own, cols), jnp.int32),
            pltpu.VMEM(tf_color.shape, jnp.float32),
            pltpu.VMEM((1, tf_extinction.shape[0]), jnp.float32),
            pltpu.VMEM(ztab.shape[1:], jnp.float32),
            pltpu.VMEM(xtab.shape[1:], jnp.float32),
            pltpu.VMEM(picker.shape, jnp.bfloat16),
            pltpu.VMEM((4 * zs, cols), jnp.bfloat16),
            pltpu.VMEM((4, 4, cols), jnp.bfloat16),
            pltpu.VMEM((4, 4, cols), jnp.bfloat16),
            pltpu.VMEM((4 * own, shifts * own), jnp.bfloat16),
            pltpu.VMEM((4 * own, shifts * 4 * zs), jnp.bfloat16),
            pltpu.VMEM((16 * xs, shifts * gathered), jnp.bfloat16),
            pltpu.VMEM((4 * own, cols), jnp.float32),
            pltpu.VMEM((4 * own, 2 * cols // bricks), jnp.float32),
            pltpu.VMEM((4, own, cols), jnp.float32),
            pltpu.VMEM((32, LANES), jnp.float32),
            pltpu.VMEM((bricks, 6 * xs, LANES), jnp.int16),
            pltpu.VMEM((bricks, 6 * xs, LANES), jnp.int16),
            pltpu.SemaphoreType.DMA((7,)),
            pltpu.SemaphoreType.REGULAR((bricks // 2 - 1,)),
            pltpu.SemaphoreType.DMA((8,)),
            pltpu.SemaphoreType.DMA((8,)),
            pltpu.SemaphoreType.DMA((bricks,)),
            pltpu.SemaphoreType.DMA((bricks,)),
        ],
        compiler_params=pltpu.CompilerParams(collective_id=0, has_side_effects=True),
        name="frame",
    )(
        density.reshape(own, cols),
        material.reshape(own, cols),
        tf_color,
        tf_extinction.reshape(1, -1),
        jnp.asarray(ztab),
        jnp.asarray(xtab),
        jnp.asarray(picker, jnp.bfloat16),
    )


def solution(mesh):
    return jax.shard_map(
        shards,
        mesh=mesh,
        in_specs=(P("depth", "plane", None), P("depth", "plane", None), P(), P()),
        out_specs=P(None, "plane", "depth"),
        check_vma=False,
    )
```
